256 devices in a mesh: tm: 64 (over x, z, core), state: 4 (over y).
Axes of the slice: x: 4, y: 4, z: 8, core: 2. Of those that a mesh axis runs over, the one named last changes fastest.
Arguments:
- generator: float32 [256, 256], replicated, may hold values from -0.03125 to 0.03125
- gates: float32 [1024, 256], P('tm'), may hold values from 0.1 to 1, as said below
- gain_rows: float32 [1024, 256], replicated, may hold values from -0.15625 to 0.15625
- obs_values: float32 [1024, 16], P('tm'), may hold values from -6 to 6
- obs_rows: int32 [1024, 16], P('tm'), may hold values from 0 to 1023
- obs_counts: int32 [1024], P('tm'), may hold values from 0 to 16, as said below
- prior_mean: float32 [256], replicated, may hold values from -6 to 6
Outputs:
- filtered: float32 [1024, 256], P('tm', 'state')
- smoothed: float32 [1024, 256], P('tm', 'state')
The draws below stay inside these ranges and needn't reach their ends.
Inputs may be any that keep to these rules, and one draw needn't show every extreme that they name: `gates`: each step's retention factors, one minus a rate that differs from state to state and from step to step, with occasional steps that drop it. `obs_counts`: some step uses all 16 slots.
All inputs are finite; a program needn't handle non-finite values.
Results may differ from the reference program's by a relative error of at most 0.0003.
Values sent between devices are 32-bit elements; how exact they have to be, the bound alone decides.
A program may use at most 128 MiB of HBM per device.

```python
import jax
import jax.numpy as jnp
from jax import lax

S = 256
OBS_ROWS = 1024
MAX_OBS = 16
HORIZON_LENGTH = 1024


def draw_gates(key, part):
    seed_collection = jax.random.split(key, 4)
    low_rate = 0.02 / HORIZON_LENGTH
    high_rate = 1.0 / 30.0
    depth_low, depth_high = (0.6, 0.8)
    poisson_intensity = jnp.exp(jax.random.uniform(seed_collection[0], (S,), jnp.float32, jnp.log(low_rate), jnp.log(high_rate)))
    rough_perturbation = jax.random.uniform(seed_collection[1], (HORIZON_LENGTH, S), jnp.float32, 0.5, 1.5)
    spike_moments = jax.random.randint(seed_collection[2], (3,), 0, HORIZON_LENGTH)
    layer_heights = jax.random.uniform(seed_collection[3], (3,), jnp.float32, depth_low, depth_high)
    instant_places = jnp.arange(HORIZON_LENGTH)
    spike_occurrences = jnp.ones((HORIZON_LENGTH,), jnp.float32)
    for other_ordinal in range(3):
        spike_occurrences = spike_occurrences * jnp.where(instant_places == spike_moments[other_ordinal], layer_heights[other_ordinal], 1.0)
    return (jnp.exp(-poisson_intensity[None, :] * rough_perturbation) * spike_occurrences[:, None]).astype(jnp.float32)


def draw_obs_counts(key, part):
    seed_collection = jax.random.split(key, 2)
    counts = jax.random.randint(seed_collection[0], (HORIZON_LENGTH,), 0, MAX_OBS + 1)
    full_spot = jax.random.randint(seed_collection[1], (), 0, HORIZON_LENGTH)
    return jnp.where(jnp.arange(HORIZON_LENGTH) == full_spot, MAX_OBS, counts).astype(jnp.int32)


def place_ends(values, stream_key, least, largest):
    shape = values.shape
    spot = [jax.random.randint(jax.random.fold_in(stream_key, axis), (), 0, shape[axis]) for axis in range(len(shape))]
    values = values.at[tuple(spot)].set(least)
    longest = shape.index(max(shape))
    spot[longest] = (spot[longest] + 1) % shape[longest]
    return values.at[tuple(spot)].set(largest)


def steps_of(own_key, extent, cuts, smallest, top_value):
    loudness = 1.0
    for position, parts in cuts:
        heights = jax.random.uniform(jax.random.fold_in(jax.random.fold_in(own_key, 6), position), (parts,), jnp.float32, smallest / len(cuts), top_value / len(cuts))
        loudness = loudness * jnp.repeat(jnp.exp(heights), extent[position] // parts).reshape((-1,) + (1,) * (len(extent) - 1 - position))
    return loudness


def centred(rng, shape, deviation, reach, cuts=(), kind=jnp.bfloat16):
    factor_of = steps_of(rng, shape, cuts, -0.22, 0.18) if cuts else 1.0
    drawn = jax.random.normal(rng, shape, jnp.float32) * deviation * factor_of
    return jnp.minimum(jnp.maximum(drawn, -reach), reach).astype(kind)


def setup_inputs(seed: int = 0) -> dict:
    arg_keys = jax.random.split(jax.random.key(seed), 8)
    return {
        "generator": centred(arg_keys[0], (S, S), (0.1 / (8 * S) ** 0.5), 0.03125, (), jnp.float32),
        "gates": draw_gates(jax.random.fold_in(arg_keys[7], 71), 0),
        "gain_rows": centred(arg_keys[2], (OBS_ROWS, S), ((2.0 / (MAX_OBS * HORIZON_LENGTH)) ** 0.5), 0.15625, (), jnp.float32),
        "obs_values": centred(arg_keys[3], (HORIZON_LENGTH, MAX_OBS), 1.0, 6.0, ((0, 64),), jnp.float32),
        "obs_rows": place_ends(jax.random.randint(arg_keys[4], (HORIZON_LENGTH, MAX_OBS), 0, OBS_ROWS), jax.random.fold_in(arg_keys[4], 1), 0, OBS_ROWS - 1).astype(jnp.int32),
        "obs_counts": draw_obs_counts(jax.random.fold_in(arg_keys[7], 71), 0),
        "prior_mean": centred(arg_keys[6], (S,), 1.0, 6.0, (), jnp.float32),
    }


def build_transition(generator):
    skew_part = generator - generator.T
    identity_matrix = jnp.eye(S, dtype=jnp.float32)
    return identity_matrix + skew_part + 0.5 * jnp.dot(skew_part, skew_part, precision=lax.Precision.HIGHEST)


def reference(generator, gates, gain_rows, obs_values, obs_rows, obs_counts, prior_mean):
    transition = build_transition(generator)
    inputs = jnp.zeros((HORIZON_LENGTH, S), jnp.float32)
    for slot_idx in range(MAX_OBS):
        active = slot_idx < obs_counts
        weight = jnp.where(active, obs_values[:, slot_idx], 0.0)
        inputs = inputs + weight[:, None] * gain_rows[obs_rows[:, slot_idx]]

    def forward_step(current, pieces):
        gate_row, input_row = pieces
        current = gate_row * jnp.dot(transition, current, precision=lax.Precision.HIGHEST) + input_row
        return current, current

    unused, filtered = lax.scan(forward_step, prior_mean, (gates, inputs))
    next_gates = jnp.concatenate([gates[1:], jnp.zeros((1, S), jnp.float32)], 0)
    predicted = jnp.dot(filtered, transition.T, precision=lax.Precision.HIGHEST)
    offsets = filtered - jnp.dot(next_gates * next_gates * predicted, transition, precision=lax.Precision.HIGHEST)

    def backward_step(current, pieces):
        gate_row, offset_row = pieces
        current = jnp.dot(gate_row * current, transition, precision=lax.Precision.HIGHEST) + offset_row
        return current, current

    unused_two, smoothed = lax.scan(backward_step, jnp.zeros((S,), jnp.float32), (next_gates, offsets), reverse=True)
    return (filtered, smoothed)
```

```python
import jax
import jax.numpy as jnp
from jax import lax
from jax.experimental import pallas as pl
from jax.experimental.pallas import tpu as pltpu
from jax.sharding import Mesh
from jax.sharding import PartitionSpec as P

TM = ("x", "z", "c")
NX, NZ, NC, NY = 4, 8, 2, 4
S = 256
STEPS = 16
QUADS = 4
ROWS = S + 8
BLOCK = 64
BROWS = BLOCK + 8


def split(x):
    hi = x.astype(jnp.bfloat16)
    return hi, (x - hi.astype(jnp.float32)).astype(jnp.bfloat16)


def mm(a, b):
    return jnp.dot(a, b, preferred_element_type=jnp.float32)


def dot3(a, b):
    ah, al = split(a)
    bh, bl = b
    return mm(ah, bh) + mm(al, bh) + mm(ah, bl)


def eye_mask(rows, first):
    r = lax.broadcasted_iota(jnp.int32, (rows, S), 0) + first
    return r == lax.broadcasted_iota(jnp.int32, (rows, S), 1)


def to_col(row, rows, first):
    return jnp.sum(jnp.where(eye_mask(rows, first), row, 0.0), axis=1, keepdims=True)


def to_row(col, first):
    return jnp.sum(jnp.where(eye_mask(col.shape[0], first), col, 0.0), axis=0, keepdims=True)


def step_on(blocks, row, add):
    out = add
    for first, t in blocks:
        out = out + jnp.sum(t * to_col(row, t.shape[0], first), axis=0, keepdims=True)
    return out


def step_back(blocks, row, add):
    out = add
    for first, t in blocks:
        out = out + to_row(jnp.sum(t * row, axis=1, keepdims=True), first)
    return out


def kernel(
    gen_ref, gates_ref, gain_ref, vals_ref, rows_ref, counts_ref, prior_ref,
    filt_ref, smooth_ref,
    weights, u_s, cur, acc, quad, plane, vecs, hist_f, hist_e, chain_out,
    send_a, recv_a, send_b, recv_b, send_c, recv_c, send_d, recv_d,
):
    x, z, c, y = (lax.axis_index(a) for a in ("x", "z", "c", "y"))
    zb = lax.rem(z, 2)
    pos = zb * 2 + c
    mine = z // 2
    sib = 1 - c
    zpair = z + 1 - 2 * zb

    def dev(dx=None, dz=None, dc=None):
        return (x if dx is None else dx, z if dz is None else dz, c if dc is None else dc, y)

    MESH = pl.DeviceIdType.MESH
    barrier = pltpu.get_barrier_semaphore()
    pl.semaphore_signal(barrier, inc=1, device_id=dev(dc=sib), device_id_type=MESH)
    for k in range(1, NZ):
        pl.semaphore_signal(barrier, inc=1, device_id=dev(dz=lax.rem(z + k, NZ)), device_id_type=MESH)
    for k in (1, NX - 1):
        pl.semaphore_signal(barrier, inc=1, device_id=dev(dx=lax.rem(x + k, NX)), device_id_type=MESH)

    gen = gen_ref[...]
    skew = gen - gen.T
    sq = dot3(skew, split(skew))
    eye = jnp.where(eye_mask(S, 0), 1.0, 0.0)
    at = eye - skew + 0.5 * sq
    a = eye + skew + 0.5 * sq
    weights[0], weights[1] = split(at)
    weights[2], weights[3] = split(a)

    slots = vals_ref.shape[1]
    sensors = gain_ref.shape[0]
    lane = lax.broadcasted_iota(jnp.int32, (STEPS, slots), 1)
    line = lax.broadcasted_iota(jnp.int32, (STEPS, slots), 0)
    count = jnp.zeros((STEPS, slots), jnp.int32)
    for t in range(STEPS):
        count = jnp.where(line == t, counts_ref[t], count)
    vals = jnp.where(lane < count, vals_ref[...], 0.0)
    rows = rows_ref[...]
    ids = lax.broadcasted_iota(jnp.int32, (STEPS, sensors), 1)
    w = jnp.zeros((STEPS, sensors), jnp.float32)
    for s in range(slots):
        w = w + jnp.where(rows[:, s : s + 1] == ids, vals[:, s : s + 1], 0.0)
    u_s[...] = dot3(w, split(gain_ref[...]))

    g0 = gates_ref[0:1, :]
    u0 = u_s[0:1, :]
    first = g0 * at
    cur[0:S, :] = first
    cur[S:, :] = jnp.broadcast_to(u0, (16, S))
    acc[...] = first * u0

    def advance(t, _):
        g = gates_ref[pl.ds(t, 1), :]
        u = u_s[pl.ds(t, 1), :]
        w_at = (weights[0], weights[1])
        new = g * dot3(cur[...], w_at)
        body = new[0:S]
        cur[0:S, :] = body
        cur[S:, :] = new[S:] + u
        acc[...] = acc[...] + body * u
        return 0

    lax.fori_loop(1, STEPS, advance, 0)
    back = to_row(jnp.sum(acc[...], axis=1, keepdims=True), 0)
    own = quad.at[pos]
    own[0:S, :] = cur[0:S, :]
    own[S : S + 1, :] = cur[S : S + 1, :]
    own[S + 1 : S + 2, :] = back

    pl.semaphore_wait(barrier, 10)

    def copy(src, dst, ssem, rsem, to):
        return pltpu.make_async_remote_copy(
            src_ref=src, dst_ref=dst, send_sem=ssem, recv_sem=rsem, device_id=to, device_id_type=MESH
        )

    far = (1 - zb) * 2 + c
    a0 = copy(own, own, send_a.at[0], recv_a.at[0], dev(dc=sib))
    a1 = copy(own, own, send_a.at[1], recv_a.at[1], dev(dz=zpair))
    a1.start()
    a0.start()
    a1.wait_recv()
    a2 = copy(quad.at[far], quad.at[far], send_a.at[2], recv_a.at[2], dev(dc=sib))
    a2.start()
    a0.wait_recv()
    a2.wait_recv()

    start = pl.multiple_of(pos * BLOCK, BLOCK)
    part = quad[0, pl.ds(start, BLOCK), :]
    for k in range(1, 4):
        part = dot3(part, split(quad[k, 0:S, :]))
    vq = quad[0, S : S + 1, :]
    bq = quad[3, S + 1 : S + 2, :]
    for k in range(1, 4):
        vq = step_on([(0, quad[k, 0:S, :])], vq, quad[k, S : S + 1, :])
        n = 3 - k
        bq = step_back([(0, quad[n, 0:S, :])], bq, quad[n, S + 1 : S + 2, :])
    block = plane.at[mine, pos]
    block[0:BLOCK, :] = part
    block[BLOCK : BLOCK + 1, :] = vq
    block[BLOCK + 1 : BLOCK + 2, :] = bq

    outgoing = []
    for k in (4, 3, 5, 2, 6, 1, 7):
        d = copy(block, block, send_b.at[k - 1], recv_b.at[k - 1], dev(dz=lax.rem(z + k, NZ)))
        d.start()
        outgoing.append(d)
    d0 = copy(block, block, send_c.at[0], recv_c.at[0], dev(dc=sib))
    d0.start()
    forwards = [d0]
    for k in (1, 7, 2, 6, 3, 5, 4):
        zs = lax.rem(z + NZ - k, NZ)
        got = plane.at[zs // 2, lax.rem(zs, 2) * 2 + c]
        copy(got, got, send_b.at[k - 1], recv_b.at[k - 1], dev(dz=lax.rem(z + k, NZ))).wait_recv()
        f = copy(got, got, send_c.at[k], recv_c.at[k], dev(dc=sib))
        f.start()
        forwards.append(f)
    for f in forwards:
        f.wait_recv()

    def plane_blocks(q):
        return [(k * BLOCK, plane[q, k, 0:BLOCK, :]) for k in range(4)]

    def forward():
        @pl.when(x > 0)
        def _():
            copy(chain_out.at[0], vecs.at[0], send_d.at[0], recv_d.at[0], dev(dx=lax.rem(x + 1, NX))).wait_recv()

        row = jnp.where(x > 0, vecs[0, 0:1, :], prior_ref[...])
        for q in range(QUADS):
            hist_f[q : q + 1, :] = row
            row = step_on(plane_blocks(q), row, plane[q, 0, BLOCK : BLOCK + 1, :])
        chain_out[0] = jnp.broadcast_to(row, (8, S))

        @pl.when(x < NX - 1)
        def _():
            copy(chain_out.at[0], vecs.at[0], send_d.at[0], recv_d.at[0], dev(dx=lax.rem(x + 1, NX))).start()

    def backward():
        @pl.when(x < NX - 1)
        def _():
            copy(chain_out.at[1], vecs.at[1], send_d.at[1], recv_d.at[1], dev(dx=lax.rem(x + 1, NX))).wait_recv()

        row = jnp.where(x < NX - 1, vecs[1, 0:1, :], jnp.zeros((1, S), jnp.float32))
        for q in reversed(range(QUADS)):
            hist_e[q : q + 1, :] = row
            row = step_back(plane_blocks(q), row, plane[q, 0, BLOCK + 1 : BLOCK + 2, :])
        chain_out[1] = jnp.broadcast_to(row, (8, S))

        @pl.when(x > 0)
        def _():
            copy(chain_out.at[1], vecs.at[1], send_d.at[1], recv_d.at[1], dev(dx=lax.rem(x + NX - 1, NX))).start()

    @pl.when(x < 2)
    def _():
        forward()
        backward()

    @pl.when(x >= 2)
    def _():
        backward()
        forward()

    f_in = hist_f[pl.ds(mine, 1), :]
    e_in = hist_e[pl.ds(mine, 1), :]
    for k in range(3):
        f_new = step_on([(0, quad[k, 0:S, :])], f_in, quad[k, S : S + 1, :])
        f_in = jnp.where(k < pos, f_new, f_in)
        n = 3 - k
        e_new = step_back([(0, quad[n, 0:S, :])], e_in, quad[n, S + 1 : S + 2, :])
        e_in = jnp.where(n > pos, e_new, e_in)

    f = jnp.broadcast_to(f_in, (16, S))
    e = jnp.broadcast_to(e_in, (16, S))
    hist_f[...] = jnp.zeros((STEPS, S), jnp.float32)
    hist_e[STEPS - 1 : STEPS, :] = e_in
    w_at = (weights[0], weights[1])
    w_a = (weights[2], weights[3])
    for t in range(STEPS):
        f = gates_ref[t : t + 1, :] * dot3(f, w_at) + u_s[t : t + 1, :]
        hist_f[t : t + 1, :] = f[0:1, :]
        r = STEPS - 1 - t
        if r > 0:
            e = dot3((e + u_s[r : r + 1, :]) * gates_ref[r : r + 1, :], w_a)
            hist_e[r - 1 : r, :] = e[0:1, :]
    fh = hist_f[...]
    sh = fh + hist_e[...]
    width = S // NY
    fo = fh[:, 0:width]
    so = sh[:, 0:width]
    for k in range(1, NY):
        fo = jnp.where(y == k, fh[:, k * width : (k + 1) * width], fo)
        so = jnp.where(y == k, sh[:, k * width : (k + 1) * width], so)
    filt_ref[...] = fo
    smooth_ref[...] = so

    a0.wait_send()
    a1.wait_send()
    a2.wait_send()
    for d in outgoing:
        d.wait_send()
    for f in forwards:
        f.wait_send()

    @pl.when(x < NX - 1)
    def _():
        copy(chain_out.at[0], vecs.at[0], send_d.at[0], recv_d.at[0], dev(dx=lax.rem(x + 1, NX))).wait_send()

    @pl.when(x > 0)
    def _():
        copy(chain_out.at[1], vecs.at[1], send_d.at[1], recv_d.at[1], dev(dx=lax.rem(x + 1, NX))).wait_send()


def shards(generator, gates, gain_rows, obs_values, obs_rows, obs_counts, prior_mean):
    width = S // NY
    vmem = pl.BlockSpec(memory_space=pltpu.VMEM)
    smem = pl.BlockSpec(memory_space=pltpu.SMEM)
    f32 = jnp.float32
    dma = pltpu.SemaphoreType.DMA
    return pl.pallas_call(
        kernel,
        out_shape=[jax.ShapeDtypeStruct((STEPS, width), f32)] * 2,
        in_specs=[vmem] * 5 + [smem, vmem],
        out_specs=[vmem] * 2,
        scratch_shapes=[
            pltpu.VMEM((4, S, S), jnp.bfloat16),
            pltpu.VMEM((STEPS, S), f32),
            pltpu.VMEM((S + 16, S), f32),
            pltpu.VMEM((S, S), f32),
            pltpu.VMEM((4, ROWS, S), f32),
            pltpu.VMEM((QUADS, 4, BROWS, S), f32),
            pltpu.VMEM((2, 8, S), f32),
            pltpu.VMEM((STEPS, S), f32),
            pltpu.VMEM((STEPS, S), f32),
            pltpu.VMEM((2, 8, S), f32),
            dma((3,)), dma((3,)),
            dma((7,)), dma((7,)),
            dma((8,)), dma((8,)),
            dma((2,)), dma((2,)),
        ],
        compiler_params=pltpu.CompilerParams(collective_id=0, has_side_effects=True),
    )(generator, gates, gain_rows, obs_values, obs_rows, obs_counts, prior_mean.reshape(1, S))


def solution(mesh):
    finer = Mesh(mesh.devices.reshape(NX, NZ, NC, NY), TM + ("y",))
    in_specs = (P(), P(TM, None), P(), P(TM, None), P(TM, None), P(TM), P())
    out_specs = (P(TM, "y"), P(TM, "y"))
    return jax.shard_map(shards, mesh=finer, in_specs=in_specs, out_specs=out_specs, check_vma=False)
```

```python
import jax
import jax.numpy as jnp
from jax import lax
from jax.experimental import pallas as pl
from jax.experimental.pallas import tpu as pltpu
from jax.sharding import Mesh
from jax.sharding import PartitionSpec as P

TM = ("x", "z", "c")
NX, NZ, NC, NY = 4, 8, 2, 4
S = 256
STEPS = 16
ROWS = S + 8
HALF = S // 2
PART = HALF // 4


def split(x):
    hi = x.astype(jnp.bfloat16)
    return hi, (x - hi.astype(jnp.float32)).astype(jnp.bfloat16)


def mm(a, b):
    return jnp.dot(a, b, preferred_element_type=jnp.float32)


def dot3(a, b):
    ah, al = split(a)
    bh, bl = b
    return mm(ah, bh) + mm(al, bh) + mm(ah, bl)


def eye_mask(rows, first):
    r = lax.broadcasted_iota(jnp.int32, (rows, S), 0) + first
    return r == lax.broadcasted_iota(jnp.int32, (rows, S), 1)


def to_col(row, rows, first):
    return jnp.sum(jnp.where(eye_mask(rows, first), row, 0.0), axis=1, keepdims=True)


def to_row(col, first):
    return jnp.sum(jnp.where(eye_mask(col.shape[0], first), col, 0.0), axis=0, keepdims=True)


def step_on(t, row, add):
    return jnp.sum(t * to_col(row, S, 0), axis=0, keepdims=True) + add


def step_back(t, row, add):
    return to_row(jnp.sum(t * row, axis=1, keepdims=True), 0) + add


def kernel(
    gen_hbm, gates_hbm, gain_hbm, vals_hbm, rows_hbm, counts_ref, prior_ref,
    out_ref,
    gen_ref, gates_ref, gain_ref, vals_ref, rows_ref,
    weights, u_s, cur, acc, hist_f, hist_b, pair, plane, vecs, ends, enter_f, enter_e, chain_out,
    in_sem, send_a, recv_a, send_z, recv_z, send_y, recv_y, send_c, recv_c, send_v, recv_v, send_d, recv_d,
):
    x, z, c, y = (lax.axis_index(a) for a in ("x", "z", "c", "y"))
    sib = 1 - c
    right, left = lax.rem(z + 1, NZ), lax.rem(z + NZ - 1, NZ)
    above, below = lax.rem(y + 1, NY), lax.rem(y + NY - 1, NY)
    MESH = pl.DeviceIdType.MESH

    def dev(dx=None, dz=None, dc=None, dy=None):
        return tuple(a if d is None else d for a, d in ((x, dx), (z, dz), (c, dc), (y, dy)))

    barrier = pltpu.get_barrier_semaphore()
    partners = [dev(dc=sib), dev(dy=above), dev(dy=below)]
    partners += [dev(dz=lax.rem(z + k, NZ)) for k in range(1, NZ)]
    partners += [dev(dx=lax.rem(x + k, NX)) for k in (1, NX - 1)]
    for to in partners:
        pl.semaphore_signal(barrier, inc=1, device_id=to, device_id_type=MESH)

    loads = [
        pltpu.make_async_copy(src, dst, in_sem.at[k])
        for k, (src, dst) in enumerate(
            ((gen_hbm, gen_ref), (rows_hbm, rows_ref), (vals_hbm, vals_ref), (gates_hbm, gates_ref), (gain_hbm, gain_ref))
        )
    ]
    for load in loads:
        load.start()

    loads[0].wait()
    gen = gen_ref[...]
    skew = gen - gen.T
    half_sq = 0.5 * dot3(skew, split(skew))
    eye = jnp.where(eye_mask(S, 0), 1.0, 0.0)
    dt = half_sq - skew
    weights[0], weights[1] = split(dt)
    weights[2], weights[3] = split(half_sq + skew)

    loads[1].wait()
    loads[2].wait()
    slots = vals_ref.shape[1]
    sensors = gain_ref.shape[0]
    lane = lax.broadcasted_iota(jnp.int32, (STEPS, slots), 1)
    line = lax.broadcasted_iota(jnp.int32, (STEPS, slots), 0)
    count = jnp.zeros((STEPS, slots), jnp.int32)
    for t in range(STEPS):
        count = jnp.where(line == t, counts_ref[t], count)
    vals = jnp.where(lane < count, vals_ref[...], 0.0)
    rows = rows_ref[...]
    ids = lax.broadcasted_iota(jnp.int32, (STEPS, sensors), 1)
    w = jnp.zeros((STEPS, sensors), jnp.float32)
    for s in range(slots):
        w = w + jnp.where(rows[:, s : s + 1] == ids, vals[:, s : s + 1], 0.0)
    loads[3].wait()
    loads[4].wait()
    u_s[...] = dot3(w, split(gain_ref[...]))

    lanes = pl.ds(pl.multiple_of((y // 2) * 128, 128), 128)

    def keep(hist, t):
        hist[t] = cur[0:ROWS, lanes]

    first = gates_ref[0:1, :] * (eye + dt)
    u0 = u_s[0:1, :]
    cur[0:S, :] = first
    cur[S:, :] = jnp.broadcast_to(u0, (16, S))
    acc[...] = first * u0
    keep(hist_f, 0)

    def advance(t, _):
        g = gates_ref[pl.ds(t, 1), :]
        u = u_s[pl.ds(t, 1), :]
        old = cur[...]
        new = g * (old + dot3(old, (weights[0], weights[1])))
        body = new[0:S]
        cur[0:S, :] = body
        cur[S:, :] = new[S:] + u
        acc[...] = acc[...] + body * u
        keep(hist_f, t)
        return 0

    lax.fori_loop(1, STEPS, advance, 0)
    own = pair.at[c]
    own[0 : S + 8, :] = cur[0 : S + 8, :]
    own[S + 1 : S + 2, :] = to_row(jnp.sum(acc[...], axis=1, keepdims=True), 0)

    pl.semaphore_wait(barrier, len(partners))

    def copy(src, dst, ssem, rsem, to):
        return pltpu.make_async_remote_copy(
            src_ref=src, dst_ref=dst, send_sem=ssem, recv_sem=rsem, device_id=to, device_id_type=MESH
        )

    sent = []

    def go(*args):
        d = copy(*args)
        d.start()
        sent.append(d)

    swap = copy(own, own, send_a, recv_a, dev(dc=sib))
    swap.start()
    sent.append(swap)
    swap.wait_recv()
    base = pl.multiple_of(c * HALF, HALF)
    plane[z, pl.ds(base, HALF), :] = dot3(pair[0, pl.ds(base, HALF), :], split(pair[1, 0:S, :]))

    def part(zs, k):
        return plane.at[zs, pl.ds(pl.multiple_of(c * HALF + k * PART, PART), PART), :]

    part_a, part_b = y, above
    part_c, part_d = below, lax.rem(y + 2, NY)
    kinds = (part_a, part_b, part_c, part_d)

    def ring(way, step, kind, zs):
        ref = part(zs, kinds[kind])
        return ref, ref, send_z.at[way, step - 1, kind], recv_z.at[way, step - 1, kind], dev(dz=left if way else right)

    for kind in (0, 1):
        for way in (0, 1):
            go(*ring(way, 1, kind, z))
    mine = plane.at[z, pl.ds(base, HALF), :]
    go(mine, mine, send_c.at[7, 0], recv_c.at[7, 0], dev(dc=sib))
    t1 = pair[1, 0:S, :]
    vecs[z, 0:1, :] = step_on(t1, pair[0, S : S + 1, :], pair[1, S : S + 1, :])
    vecs[z, 1:2, :] = step_back(pair[0, 0:S, :], pair[1, S + 1 : S + 2, :], pair[0, S + 1 : S + 2, :])
    for k in range(1, NZ):
        go(vecs.at[z], vecs.at[z], send_v.at[k - 1], recv_v.at[k - 1], dev(dz=lax.rem(z + k, NZ)))

    def reset():
        cur[0:S, :] = eye
        cur[S:, :] = jnp.zeros((16, S), jnp.float32)

    def retreat(k, _):
        t = STEPS - 1 - k
        g = gates_ref[pl.ds(t, 1), :]
        u = u_s[pl.ds(t, 1), :]
        cur[S:, :] = cur[S:, :] + u
        old = cur[...] * g
        cur[...] = old + dot3(old, (weights[2], weights[3]))
        keep(hist_b, t - 1)
        return 0

    def other_y(slot, zs):
        for kind, source in ((2, 0), (3, 1)):
            ref = part(zs, kinds[kind])
            copy(ref, ref, send_y.at[slot, source], recv_y.at[slot, source], dev(dy=above)).wait_recv()
            go(ref, ref, send_c.at[slot, kind], recv_c.at[slot, kind], dev(dc=sib))

    def arrive(way, step, kind):
        zs = lax.rem(z + (step if way else NZ - step), NZ)
        args = ring(way, step, kind, zs)
        copy(*args).wait_recv()
        if step < 3 or (step == 3 and kind == way):
            go(*ring(way, step + 1, kind, zs))
        slot = 3 if step == 4 else way * 4 + step - 1
        ref = part(zs, kinds[kind])
        go(ref, ref, send_y.at[slot, kind], recv_y.at[slot, kind], dev(dy=below if kind else above))
        go(ref, ref, send_c.at[slot, kind], recv_c.at[slot, kind], dev(dc=sib))

    reset()
    lax.fori_loop(0, 5, retreat, 0)
    waiting = []
    done = 5
    for step in (1, 2, 3, 4):
        for kind in (0, 1):
            for way in (0, 1):
                if step < 4 or kind == way:
                    arrive(way, step, kind)
        for slot, zs in waiting:
            other_y(slot, zs)
        if step == 4:
            waiting = [(3, lax.rem(z + 4, NZ))]
        else:
            waiting = [(step - 1, lax.rem(z + NZ - step, NZ)), (4 + step - 1, lax.rem(z + step, NZ))]
            more = min(STEPS - 1, done + 4)
            lax.fori_loop(done, more, retreat, 0)
            done = more
    for slot, zs in waiting:
        other_y(slot, zs)
    for k in range(1, NZ):
        v = vecs.at[z]
        copy(v, v, send_v.at[k - 1], recv_v.at[k - 1], dev(dz=right)).wait_recv()
    whole = plane.at[z, pl.ds(0, HALF), :]
    copy(whole, whole, send_c.at[7, 0], recv_c.at[7, 0], dev(dc=sib)).wait_recv()
    quarter = plane.at[z, pl.ds(0, PART), :]
    for slot in range(7):
        for kind in range(4):
            copy(quarter, quarter, send_c.at[slot, kind], recv_c.at[slot, kind], dev(dc=sib)).wait_recv()

    def chain(way, to):
        return copy(chain_out.at[way], ends.at[way], send_d.at[way], recv_d.at[way], dev(dx=to))

    after, before = lax.rem(x + 1, NX), lax.rem(x + NX - 1, NX)

    def forward():
        @pl.when(x > 0)
        def _():
            chain(0, after).wait_recv()

        row = jnp.where(x > 0, ends[0, 0:1, :], prior_ref[...])
        for k in range(NZ):
            enter_f[k : k + 1, :] = row
            row = step_on(plane[k], row, vecs[k, 0:1, :])
        chain_out[0] = jnp.broadcast_to(row, (8, S))

        @pl.when(x < NX - 1)
        def _():
            chain(0, after).start()

    def backward():
        @pl.when(x < NX - 1)
        def _():
            chain(1, before).wait_recv()

        row = jnp.where(x < NX - 1, ends[1, 0:1, :], jnp.zeros((1, S), jnp.float32))
        for k in reversed(range(NZ)):
            enter_e[k : k + 1, :] = row
            row = step_back(plane[k], row, vecs[k, 1:2, :])
        chain_out[1] = jnp.broadcast_to(row, (8, S))

        @pl.when(x > 0)
        def _():
            chain(1, before).start()

    @pl.when(x < 2)
    def _():
        forward()
        backward()

    @pl.when(x >= 2)
    def _():
        backward()
        forward()

    f_in = enter_f[pl.ds(z, 1), :]
    e_in = enter_e[pl.ds(z, 1), :]
    f_in = jnp.where(c == 1, step_on(pair[0, 0:S, :], f_in, pair[0, S : S + 1, :]), f_in)
    e_in = jnp.where(c == 0, step_back(pair[1, 0:S, :], e_in, pair[1, S + 1 : S + 2, :]), e_in)
    f_col = to_col(f_in, S, 0)
    e_col = to_col(e_in, S, 0)
    width = S // NY
    low = lax.rem(y, 2) == 0
    e_last = jnp.where(y < 2, e_in[:, 0:128], e_in[:, 128:])

    def pick(r):
        return jnp.where(low, r[:, 0:width], r[:, width:])

    for t in range(STEPS):
        f = jnp.sum(hist_f[t, 0:S, :] * f_col, axis=0, keepdims=True) + hist_f[t, S : S + 1, :]
        if t < STEPS - 1:
            e = jnp.sum(hist_b[t, 0:S, :] * e_col, axis=0, keepdims=True) + hist_b[t, S : S + 1, :]
        else:
            e = e_last
        out_ref[t : t + 1, :] = pick(f)
        out_ref[STEPS + t : STEPS + t + 1, :] = pick(f + e)

    for d in sent:
        d.wait_send()

    @pl.when(x < NX - 1)
    def _():
        chain(0, after).wait_send()

    @pl.when(x > 0)
    def _():
        chain(1, before).wait_send()


def part_results(both_ref, filt_ref, smooth_ref):
    filt_ref[...] = both_ref[0:STEPS, :]
    smooth_ref[...] = both_ref[STEPS:, :]


def shards(generator, gates, gain_rows, obs_values, obs_rows, obs_counts, prior_mean):
    width = S // NY
    vmem = pl.BlockSpec(memory_space=pltpu.VMEM)
    smem = pl.BlockSpec(memory_space=pltpu.SMEM)
    hbm = pl.BlockSpec(memory_space=pl.ANY)
    f32 = jnp.float32
    dma = pltpu.SemaphoreType.DMA
    inputs = (generator, gates, gain_rows, obs_values, obs_rows)
    both = pl.pallas_call(
        kernel,
        out_shape=jax.ShapeDtypeStruct((2 * STEPS, width), f32),
        in_specs=[hbm] * 5 + [smem, vmem],
        out_specs=vmem,
        scratch_shapes=[pltpu.VMEM(a.shape, a.dtype) for a in inputs]
        + [
            pltpu.VMEM((4, S, S), jnp.bfloat16),
            pltpu.VMEM((STEPS, S), f32),
            pltpu.VMEM((S + 16, S), f32),
            pltpu.VMEM((S, S), f32),
            pltpu.VMEM((STEPS, ROWS, 128), f32),
            pltpu.VMEM((STEPS, ROWS, 128), f32),
            pltpu.VMEM((2, ROWS, S), f32),
            pltpu.VMEM((NZ, S, S), f32),
            pltpu.VMEM((NZ, 2, S), f32),
            pltpu.VMEM((2, 8, S), f32),
            pltpu.VMEM((NZ, S), f32),
            pltpu.VMEM((NZ, S), f32),
            pltpu.VMEM((2, 8, S), f32),
            dma((5,)),
            dma, dma,
            dma((2, 4, 2)), dma((2, 4, 2)),
            dma((7, 2)), dma((7, 2)),
            dma((8, 4)), dma((8, 4)),
            dma((7,)), dma((7,)),
            dma((2,)), dma((2,)),
        ],
        compiler_params=pltpu.CompilerParams(collective_id=0, has_side_effects=True),
    )(*inputs, obs_counts, prior_mean.reshape(1, S))
    return pl.pallas_call(
        part_results,
        out_shape=[jax.ShapeDtypeStruct((STEPS, width), f32)] * 2,
        in_specs=[vmem],
        out_specs=[vmem] * 2,
    )(both)


def solution(mesh):
    finer = Mesh(mesh.devices.reshape(NX, NZ, NC, NY), TM + ("y",))
    in_specs = (P(), P(TM, None), P(), P(TM, None), P(TM, None), P(TM), P())
    out_specs = (P(TM, "y"), P(TM, "y"))
    return jax.shard_map(shards, mesh=finer, in_specs=in_specs, out_specs=out_specs, check_vma=False)
```

```python
import jax
import jax.numpy as jnp
from jax import lax
from jax.experimental import pallas as pl
from jax.experimental.pallas import tpu as pltpu
from jax.sharding import Mesh
from jax.sharding import PartitionSpec as P

TM = ("x", "z", "c")
NX, NZ, NC, NY = 4, 8, 2, 4
S = 256
STEPS = 16
ROWS = S + 8
HALF = S // 2
PART = HALF // 4


def split(x):
    hi = x.astype(jnp.bfloat16)
    return hi, (x - hi.astype(jnp.float32)).astype(jnp.bfloat16)


def mm(a, b):
    return jnp.dot(a, b, preferred_element_type=jnp.float32)


def dot3(a, b):
    ah, al = split(a)
    bh, bl = b
    return mm(ah, bh) + mm(al, bh) + mm(ah, bl)


def eye_mask(rows, columns):
    r = lax.broadcasted_iota(jnp.int32, (rows, columns), 0)
    return r == lax.broadcasted_iota(jnp.int32, (rows, columns), 1)


def to_col(row):
    m = eye_mask(HALF, HALF)
    cols = [jnp.sum(jnp.where(m, row[:, k : k + HALF], 0.0), axis=1, keepdims=True) for k in (0, HALF)]
    return jnp.concatenate(cols, axis=0)


def to_row(col):
    m = eye_mask(HALF, HALF)
    rows = [jnp.sum(jnp.where(m, col[k : k + HALF, :], 0.0), axis=0, keepdims=True) for k in (0, HALF)]
    return jnp.concatenate(rows, axis=1)


def step_on(t, row, add):
    return jnp.sum(t * to_col(row), axis=0, keepdims=True) + add


def step_back(t, row, add):
    return to_row(jnp.sum(t * row, axis=1, keepdims=True)) + add


def kernel(
    gen_hbm, gates_hbm, gain_hbm, vals_hbm, rows_hbm, counts_ref, prior_ref,
    out_ref,
    gen_ref, gates_ref, gain_ref, vals_ref, rows_ref,
    weights, u_s, cur, acc, hist_f, hist_b, pair, plane, vecs, ends, enter_f, enter_e, chain_out, ahead, behind,
    in_sem, send_a, recv_a, send_z, recv_z, send_y, recv_y, send_c, recv_c, send_v, recv_v, send_d, recv_d,
):
    x, z, c, y = (lax.axis_index(a) for a in ("x", "z", "c", "y"))
    sib = 1 - c
    right = lax.rem(z + 1, NZ)
    above, below, across = (lax.rem(y + k, NY) for k in (1, NY - 1, 2))
    MESH = pl.DeviceIdType.MESH

    def dev(dx=None, dz=None, dc=None, dy=None):
        return tuple(a if d is None else d for a, d in ((x, dx), (z, dz), (c, dc), (y, dy)))

    barrier = pltpu.get_barrier_semaphore()
    partners = [dev(dc=sib), dev(dy=above), dev(dy=below), dev(dy=across)]
    partners += [dev(dz=lax.rem(z + k, NZ)) for k in range(1, NZ)]
    partners += [dev(dx=lax.rem(x + k, NX)) for k in (1, NX - 1)]
    for to in partners:
        pl.semaphore_signal(barrier, inc=1, device_id=to, device_id_type=MESH)

    loads = [
        pltpu.make_async_copy(src, dst, in_sem.at[k])
        for k, (src, dst) in enumerate(
            ((gen_hbm, gen_ref), (rows_hbm, rows_ref), (vals_hbm, vals_ref), (gates_hbm, gates_ref), (gain_hbm, gain_ref))
        )
    ]
    for load in loads:
        load.start()

    loads[0].wait()
    gen = gen_ref[...]
    skew = gen - gen.T
    half_sq = 0.5 * dot3(skew, split(skew))
    eye = jnp.where(eye_mask(S, S), 1.0, 0.0)
    dt = half_sq - skew
    weights[0], weights[1] = split(dt)
    weights[2], weights[3] = split(half_sq + skew)

    loads[1].wait()
    loads[2].wait()
    slots = vals_ref.shape[1]
    sensors = gain_ref.shape[0]
    lane = lax.broadcasted_iota(jnp.int32, (STEPS, slots), 1)
    line = lax.broadcasted_iota(jnp.int32, (STEPS, slots), 0)
    count = jnp.zeros((STEPS, slots), jnp.int32)
    for t in range(STEPS):
        count = jnp.where(line == t, counts_ref[t], count)
    vals = jnp.where(lane < count, vals_ref[...], 0.0)
    rows = rows_ref[...]
    ids = lax.broadcasted_iota(jnp.int32, (STEPS, sensors), 1)
    w = jnp.zeros((STEPS, sensors), jnp.float32)
    for s in range(slots):
        w = w + jnp.where(rows[:, s : s + 1] == ids, vals[:, s : s + 1], 0.0)
    loads[3].wait()
    loads[4].wait()
    u_s[...] = dot3(w, split(gain_ref[...]))

    lanes = pl.ds(pl.multiple_of((y // 2) * 128, 128), 128)

    def keep(hist, t):
        hist[t] = cur[0:ROWS, lanes]

    first = gates_ref[0:1, :] * (eye + dt)
    u0 = u_s[0:1, :]
    cur[0:S, :] = first
    cur[S:, :] = jnp.broadcast_to(u0, (16, S))
    acc[...] = first * u0
    keep(hist_f, 0)

    def advance(t, _):
        g = gates_ref[pl.ds(t, 1), :]
        u = u_s[pl.ds(t, 1), :]
        old = cur[...]
        new = g * (old + dot3(old, (weights[0], weights[1])))
        body = new[0:S]
        cur[0:S, :] = body
        cur[S:, :] = new[S:] + u
        acc[...] = acc[...] + body * u
        keep(hist_f, t)
        return 0

    lax.fori_loop(1, STEPS, advance, 0)
    own = pair.at[c]
    own[0 : S + 8, :] = cur[0 : S + 8, :]
    own[S + 1 : S + 2, :] = to_row(jnp.sum(acc[...], axis=1, keepdims=True))

    pl.semaphore_wait(barrier, len(partners))

    def copy(src, dst, ssem, rsem, to):
        return pltpu.make_async_remote_copy(
            src_ref=src, dst_ref=dst, send_sem=ssem, recv_sem=rsem, device_id=to, device_id_type=MESH
        )

    sent = []

    def go(*args):
        d = copy(*args)
        d.start()
        sent.append(d)

    swap = copy(own, own, send_a, recv_a, dev(dc=sib))
    swap.start()
    sent.append(swap)
    swap.wait_recv()
    base = pl.multiple_of(c * HALF, HALF)
    plane[z, pl.ds(base, HALF), :] = dot3(pair[0, pl.ds(base, HALF), :], split(pair[1, 0:S, :]))

    def part(zs, k):
        return plane.at[zs, pl.ds(pl.multiple_of(c * HALF + k * PART, PART), PART), :]

    kinds = (y, above, below, across)
    carried = {1: 4, 2: 2, 3: 1, 4: 1, 5: 1, 6: 2, 7: 4}

    def pieces(k, zs):
        if carried[k] == 4:
            return [(plane.at[zs, pl.ds(base, HALF), :], 0)]
        return [(part(zs, kinds[kind]), kind) for kind in range(carried[k])]

    for k in (4, 3, 5, 2, 6, 1, 7):
        for ref, i in pieces(k, z):
            go(ref, ref, send_z.at[k - 1, i], recv_z.at[k - 1, i], dev(dz=lax.rem(z + k, NZ)))
    mine = plane.at[z, pl.ds(base, HALF), :]
    go(mine, mine, send_c.at[0, 0], recv_c.at[0, 0], dev(dc=sib))
    t1 = pair[1, 0:S, :]
    vecs[z, 0:1, :] = step_on(t1, pair[0, S : S + 1, :], pair[1, S : S + 1, :])
    vecs[z, 1:2, :] = step_back(pair[0, 0:S, :], pair[1, S + 1 : S + 2, :], pair[0, S + 1 : S + 2, :])
    for k in range(1, NZ):
        go(vecs.at[z], vecs.at[z], send_v.at[k - 1], recv_v.at[k - 1], dev(dz=lax.rem(z + k, NZ)))

    cur[0:S, :] = eye
    cur[S:, :] = jnp.zeros((16, S), jnp.float32)

    def retreat(k, _):
        t = STEPS - 1 - k
        g = gates_ref[pl.ds(t, 1), :]
        u = u_s[pl.ds(t, 1), :]
        cur[S:, :] = cur[S:, :] + u
        old = cur[...] * g
        cur[...] = old + dot3(old, (weights[2], weights[3]))
        keep(hist_b, t - 1)
        return 0

    lax.fori_loop(0, STEPS - 1, retreat, 0)

    def arrive(k):
        zs = lax.rem(z + NZ - k, NZ)
        for ref, i in pieces(k, zs):
            copy(ref, ref, send_z.at[k - 1, i], recv_z.at[k - 1, i], dev(dz=right)).wait_recv()
            if carried[k] == 2:
                goals = ((2, above),) if i == 0 else ((3, below),)
            elif carried[k] == 1:
                goals = ((3, across), (2, above), (1, below))
            else:
                goals = ()
            for kind, to in goals:
                go(ref, ref, send_y.at[k - 1, kind], recv_y.at[k - 1, kind], dev(dy=to))
            go(ref, ref, send_c.at[k, i], recv_c.at[k, i], dev(dc=sib))

    def arrive_y(k):
        zs = lax.rem(z + NZ - k, NZ)
        for kind in range(carried[k], 4):
            ref = part(zs, kinds[kind])
            copy(ref, ref, send_y.at[k - 1, kind], recv_y.at[k - 1, kind], dev(dy=above)).wait_recv()
            go(ref, ref, send_c.at[k, kind], recv_c.at[k, kind], dev(dc=sib))

    for k in (4, 3, 5):
        arrive(k)
    arrive_y(4)
    for k in (2, 6):
        arrive(k)
    for k in (3, 5):
        arrive_y(k)
    for k in (1, 7):
        arrive(k)
    for k in (2, 6):
        arrive_y(k)
    for k in range(1, NZ):
        v = vecs.at[z]
        copy(v, v, send_v.at[k - 1], recv_v.at[k - 1], dev(dz=right)).wait_recv()
    whole = plane.at[z, pl.ds(0, HALF), :]
    quarter = plane.at[z, pl.ds(0, PART), :]
    copy(whole, whole, send_c.at[0, 0], recv_c.at[0, 0], dev(dc=sib)).wait_recv()
    for k in range(1, NZ):
        for i in range(1 if carried[k] == 4 else 4):
            ref = whole if carried[k] == 4 else quarter
            copy(ref, ref, send_c.at[k, i], recv_c.at[k, i], dev(dc=sib)).wait_recv()

    def chain(way):
        to = dev(dx=lax.rem(x + (NX - 1 if way else 1), NX))
        return copy(chain_out.at[way], ends.at[way], send_d.at[way], recv_d.at[way], to)

    zero = jnp.zeros((1, S), jnp.float32)
    f_row = jnp.where(x == 0, prior_ref[...], zero)
    e_row = zero
    for k in range(NZ):
        enter_f[k : k + 1, :] = f_row
        f_row = step_on(plane[k], f_row, vecs[k, 0:1, :])
        n = NZ - 1 - k
        enter_e[n : n + 1, :] = e_row
        e_row = step_back(plane[n], e_row, vecs[n, 1:2, :])
    chain_out[0] = jnp.broadcast_to(f_row, (8, S))
    chain_out[1] = jnp.broadcast_to(e_row, (8, S))

    @pl.when(x == 0)
    def _():
        chain(0).start()

    @pl.when(x == NX - 1)
    def _():
        chain(1).start()

    cur[0:S, :] = plane[0]
    ahead[...] = eye

    def compose(k, _):
        @pl.when(k == z)
        def _():
            ahead[...] = cur[0:S, :]

        cur[0:S, :] = dot3(cur[0:S, :], split(plane[k]))
        return 0

    lax.fori_loop(1, NZ, compose, 0)

    def pass_on(way):
        chain(way).wait_recv()
        row = ends[way, 0:1, :]
        new = (step_back if way else step_on)(cur[0:S, :], row, chain_out[way, 0:1, :])
        chain_out[way] = jnp.broadcast_to(new, (8, S))
        chain(way).start()

    @pl.when(x == 1)
    def _():
        pass_on(0)

    @pl.when(x == 2)
    def _():
        pass_on(1)

    behind[...] = eye

    @pl.when(z < NZ - 1)
    def _():
        behind[...] = plane[right]

    def compose_after(k, _):
        behind[...] = dot3(behind[...], split(plane[k]))
        return 0

    lax.fori_loop(jnp.minimum(z + 2, NZ), NZ, compose_after, 0)

    @pl.when(x == 1)
    def _():
        pass_on(1)

    @pl.when(x == 2)
    def _():
        pass_on(0)

    @pl.when(x == 0)
    def _():
        chain(1).wait_recv()
        ends[0] = jnp.zeros((8, S), jnp.float32)

    @pl.when(x == NX - 1)
    def _():
        chain(0).wait_recv()
        ends[1] = jnp.zeros((8, S), jnp.float32)

    f_in = step_on(ahead[...], ends[0, 0:1, :], enter_f[pl.ds(z, 1), :])
    e_in = step_back(behind[...], ends[1, 0:1, :], enter_e[pl.ds(z, 1), :])
    f_in = jnp.where(c == 1, step_on(pair[0, 0:S, :], f_in, pair[0, S : S + 1, :]), f_in)
    e_in = jnp.where(c == 0, step_back(pair[1, 0:S, :], e_in, pair[1, S + 1 : S + 2, :]), e_in)
    f_col = to_col(f_in)
    e_col = to_col(e_in)
    width = S // NY
    low = lax.rem(y, 2) == 0
    e_last = jnp.where(y < 2, e_in[:, 0:128], e_in[:, 128:])

    def pick(r):
        return jnp.where(low, r[:, 0:width], r[:, width:])

    for t in range(STEPS):
        f = jnp.sum(hist_f[t, 0:S, :] * f_col, axis=0, keepdims=True) + hist_f[t, S : S + 1, :]
        if t < STEPS - 1:
            e = jnp.sum(hist_b[t, 0:S, :] * e_col, axis=0, keepdims=True) + hist_b[t, S : S + 1, :]
        else:
            e = e_last
        out_ref[t : t + 1, :] = pick(f)
        out_ref[STEPS + t : STEPS + t + 1, :] = pick(f + e)

    for d in sent:
        d.wait_send()

    @pl.when(x < NX - 1)
    def _():
        chain(0).wait_send()

    @pl.when(x > 0)
    def _():
        chain(1).wait_send()


def part_results(both_ref, filt_ref, smooth_ref):
    filt_ref[...] = both_ref[0:STEPS, :]
    smooth_ref[...] = both_ref[STEPS:, :]


def shards(generator, gates, gain_rows, obs_values, obs_rows, obs_counts, prior_mean):
    width = S // NY
    vmem = pl.BlockSpec(memory_space=pltpu.VMEM)
    smem = pl.BlockSpec(memory_space=pltpu.SMEM)
    hbm = pl.BlockSpec(memory_space=pl.ANY)
    f32 = jnp.float32
    dma = pltpu.SemaphoreType.DMA
    inputs = (generator, gates, gain_rows, obs_values, obs_rows)
    both = pl.pallas_call(
        kernel,
        out_shape=jax.ShapeDtypeStruct((2 * STEPS, width), f32),
        in_specs=[hbm] * 5 + [smem, vmem],
        out_specs=vmem,
        scratch_shapes=[pltpu.VMEM(a.shape, a.dtype) for a in inputs]
        + [
            pltpu.VMEM((4, S, S), jnp.bfloat16),
            pltpu.VMEM((STEPS, S), f32),
            pltpu.VMEM((S + 16, S), f32),
            pltpu.VMEM((S, S), f32),
            pltpu.VMEM((STEPS, ROWS, 128), f32),
            pltpu.VMEM((STEPS, ROWS, 128), f32),
            pltpu.VMEM((2, ROWS, S), f32),
            pltpu.VMEM((NZ, S, S), f32),
            pltpu.VMEM((NZ, 2, S), f32),
            pltpu.VMEM((2, 8, S), f32),
            pltpu.VMEM((NZ, S), f32),
            pltpu.VMEM((NZ, S), f32),
            pltpu.VMEM((2, 8, S), f32),
            pltpu.VMEM((S, S), f32),
            pltpu.VMEM((S, S), f32),
            dma((5,)),
            dma, dma,
            dma((7, 2)), dma((7, 2)),
            dma((7, 4)), dma((7, 4)),
            dma((8, 4)), dma((8, 4)),
            dma((7,)), dma((7,)),
            dma((2,)), dma((2,)),
        ],
        compiler_params=pltpu.CompilerParams(collective_id=0, has_side_effects=True),
    )(*inputs, obs_counts, prior_mean.reshape(1, S))
    return pl.pallas_call(
        part_results,
        out_shape=[jax.ShapeDtypeStruct((STEPS, width), f32)] * 2,
        in_specs=[vmem],
        out_specs=[vmem] * 2,
    )(both)


def solution(mesh):
    finer = Mesh(mesh.devices.reshape(NX, NZ, NC, NY), TM + ("y",))
    in_specs = (P(), P(TM, None), P(), P(TM, None), P(TM, None), P(TM), P())
    out_specs = (P(TM, "y"), P(TM, "y"))
    return jax.shard_map(shards, mesh=finer, in_specs=in_specs, out_specs=out_specs, check_vma=False)
```

```python
import jax
import jax.numpy as jnp
from jax import lax
from jax.experimental import pallas as pl
from jax.experimental.pallas import tpu as pltpu
from jax.sharding import Mesh
from jax.sharding import PartitionSpec as P

TM = ("x", "z", "c")
NX, NZ, NC, NY = 4, 8, 2, 4
S = 256
STEPS = 16
QUADS = 4
ROWS = S + 8
HALF = S // 2
PART = HALF // 4


def split(x):
    hi = x.astype(jnp.bfloat16)
    return hi, (x - hi.astype(jnp.float32)).astype(jnp.bfloat16)


def mm(a, b):
    return jnp.dot(a, b, preferred_element_type=jnp.float32)


def dot3(a, b):
    ah, al = split(a)
    bh, bl = b
    return mm(ah, bh) + mm(al, bh) + mm(ah, bl)


def eye_mask(rows, columns):
    r = lax.broadcasted_iota(jnp.int32, (rows, columns), 0)
    return r == lax.broadcasted_iota(jnp.int32, (rows, columns), 1)


def to_col(row):
    m = eye_mask(HALF, HALF)
    cols = [jnp.sum(jnp.where(m, row[:, k : k + HALF], 0.0), axis=1, keepdims=True) for k in (0, HALF)]
    return jnp.concatenate(cols, axis=0)


def to_row(col):
    m = eye_mask(HALF, HALF)
    rows = [jnp.sum(jnp.where(m, col[k : k + HALF, :], 0.0), axis=0, keepdims=True) for k in (0, HALF)]
    return jnp.concatenate(rows, axis=1)


def step_on(t, row, add):
    return jnp.sum(t * to_col(row), axis=0, keepdims=True) + add


def step_back(t, row, add):
    return to_row(jnp.sum(t * row, axis=1, keepdims=True)) + add


def kernel(
    gen_hbm, gates_hbm, gain_hbm, vals_hbm, rows_hbm, counts_ref, prior_ref,
    out_ref,
    gen_ref, gates_ref, gain_ref, vals_ref, rows_ref,
    weights, u_s, cur, acc, hist_f, hist_b, pair, own_pair, mate, plane, pair_vec, quad_vec, ends, enter_f, enter_e, chain_out, ahead, behind,
    in_sem, send_a, recv_a, send_m, recv_m, send_z, recv_z, send_y, recv_y, send_c, recv_c, send_v, recv_v, send_d, recv_d,
):
    x, z, c, y = (lax.axis_index(a) for a in ("x", "z", "c", "y"))
    sib = 1 - c
    zb = lax.rem(z, 2)
    quad = z // 2
    mate_z = z + 1 - 2 * zb
    above, below, across = (lax.rem(y + k, NY) for k in (1, NY - 1, 2))
    MESH = pl.DeviceIdType.MESH

    def dev(dx=None, dz=None, dc=None, dy=None):
        return tuple(a if d is None else d for a, d in ((x, dx), (z, dz), (c, dc), (y, dy)))

    barrier = pltpu.get_barrier_semaphore()
    partners = [dev(dc=sib), dev(dy=above), dev(dy=below), dev(dy=across)]
    partners += [dev(dz=lax.rem(z + k, NZ)) for k in range(1, NZ)]
    partners += [dev(dx=lax.rem(x + k, NX)) for k in (1, NX - 1)]
    for to in partners:
        pl.semaphore_signal(barrier, inc=1, device_id=to, device_id_type=MESH)

    loads = [
        pltpu.make_async_copy(src, dst, in_sem.at[k])
        for k, (src, dst) in enumerate(
            ((gen_hbm, gen_ref), (rows_hbm, rows_ref), (vals_hbm, vals_ref), (gates_hbm, gates_ref), (gain_hbm, gain_ref))
        )
    ]
    for load in loads:
        load.start()

    loads[0].wait()
    gen = gen_ref[...]
    skew = gen - gen.T
    half_sq = 0.5 * dot3(skew, split(skew))
    eye = jnp.where(eye_mask(S, S), 1.0, 0.0)
    dt = half_sq - skew
    weights[0], weights[1] = split(dt)
    weights[2], weights[3] = split(half_sq + skew)

    loads[1].wait()
    loads[2].wait()
    slots = vals_ref.shape[1]
    sensors = gain_ref.shape[0]
    lane = lax.broadcasted_iota(jnp.int32, (STEPS, slots), 1)
    line = lax.broadcasted_iota(jnp.int32, (STEPS, slots), 0)
    count = jnp.zeros((STEPS, slots), jnp.int32)
    for t in range(STEPS):
        count = jnp.where(line == t, counts_ref[t], count)
    vals = jnp.where(lane < count, vals_ref[...], 0.0)
    rows = rows_ref[...]
    ids = lax.broadcasted_iota(jnp.int32, (STEPS, sensors), 1)
    w = jnp.zeros((STEPS, sensors), jnp.float32)
    for s in range(slots):
        w = w + jnp.where(rows[:, s : s + 1] == ids, vals[:, s : s + 1], 0.0)
    loads[3].wait()
    loads[4].wait()
    u_s[...] = dot3(w, split(gain_ref[...]))

    lanes = pl.ds(pl.multiple_of((y // 2) * 128, 128), 128)

    def keep(hist, t):
        hist[t] = cur[0:ROWS, lanes]

    first = gates_ref[0:1, :] * (eye + dt)
    u0 = u_s[0:1, :]
    cur[0:S, :] = first
    cur[S:, :] = jnp.broadcast_to(u0, (16, S))
    acc[...] = first * u0
    keep(hist_f, 0)

    def advance(t, _):
        g = gates_ref[pl.ds(t, 1), :]
        u = u_s[pl.ds(t, 1), :]
        old = cur[...]
        new = g * (old + dot3(old, (weights[0], weights[1])))
        body = new[0:S]
        cur[0:S, :] = body
        cur[S:, :] = new[S:] + u
        acc[...] = acc[...] + body * u
        keep(hist_f, t)
        return 0

    lax.fori_loop(1, STEPS, advance, 0)
    own = pair.at[c]
    own[0 : S + 8, :] = cur[0 : S + 8, :]
    own[S + 1 : S + 2, :] = to_row(jnp.sum(acc[...], axis=1, keepdims=True))

    pl.semaphore_wait(barrier, len(partners))

    def copy(src, dst, ssem, rsem, to):
        return pltpu.make_async_remote_copy(
            src_ref=src, dst_ref=dst, send_sem=ssem, recv_sem=rsem, device_id=to, device_id_type=MESH
        )

    sent = []

    def go(*args):
        d = copy(*args)
        d.start()
        sent.append(d)

    swap = copy(own, own, send_a, recv_a, dev(dc=sib))
    swap.start()
    sent.append(swap)
    swap.wait_recv()
    base = pl.multiple_of(c * HALF, HALF)
    own_pair[...] = dot3(pair[0, 0:S, :], split(pair[1, 0:S, :]))

    kinds = (y, above, below, across)

    def rows_of(kind):
        return pl.ds(pl.multiple_of(c * HALF + kinds[kind] * PART, PART), PART)

    def to_mate(kind):
        return copy(
            own_pair.at[rows_of(kind), :], mate.at[rows_of(kind), :], send_m.at[kind], recv_m.at[kind], dev(dz=mate_z)
        )

    first_rows = to_mate(0)
    first_rows.start()
    sent.append(first_rows)
    pair_vec[zb, 0:1, :] = step_on(pair[1, 0:S, :], pair[0, S : S + 1, :], pair[1, S : S + 1, :])
    pair_vec[zb, 1:2, :] = step_back(pair[0, 0:S, :], pair[1, S + 1 : S + 2, :], pair[0, S + 1 : S + 2, :])
    swap_vec = copy(pair_vec.at[zb], pair_vec.at[zb], send_m.at[4], recv_m.at[4], dev(dz=mate_z))
    swap_vec.start()
    sent.append(swap_vec)

    cur[0:S, :] = eye
    cur[S:, :] = jnp.zeros((16, S), jnp.float32)

    def retreat(k, _):
        t = STEPS - 1 - k
        g = gates_ref[pl.ds(t, 1), :]
        u = u_s[pl.ds(t, 1), :]
        cur[S:, :] = cur[S:, :] + u
        old = cur[...] * g
        cur[...] = old + dot3(old, (weights[2], weights[3]))
        keep(hist_b, t - 1)
        return 0

    lax.fori_loop(0, 9, retreat, 0)

    first_rows.wait_recv()

    def others(act):
        for dq in (2, 1, 3, 0):
            for to_b in (0, 1):
                to = dev(dz=lax.rem(2 * quad + 2 * dq, NZ) + to_b)
                if dq or not to_b:
                    act(to, dq, to_b)

    def quad_rows(q, kind):
        return plane.at[q, rows_of(kind), :]

    def spread(to, dq, to_b):
        ref = quad_rows(quad, 0)
        return copy(ref, ref, send_z.at[dq, to_b], recv_z.at[(4 - dq) % 4], to)

    @pl.when(zb == 1)
    def _():
        plane[quad, rows_of(0), :] = dot3(mate[rows_of(0), :], split(own_pair[...]))
        others(lambda *a: spread(*a).start())

    for kind in (1, 2, 3):
        d = to_mate(kind)
        d.start()
        sent.append(d)

    swap_vec.wait_recv()

    @pl.when(zb == 1)
    def _():
        quad_vec[quad, 0] = step_on(own_pair[...], pair_vec[0, 0:1, :], pair_vec[1, 0:1, :])

    @pl.when(zb == 0)
    def _():
        quad_vec[quad, 1] = step_back(own_pair[...], pair_vec[1, 1:2, :], pair_vec[0, 1:2, :])

    def spread_vec(to_z, dq, far):
        ref = quad_vec.at[quad, 1 - zb]
        return copy(ref, ref, send_v.at[dq, far], recv_v.at[(4 - dq) % 4, 1 - zb], dev(dz=to_z))

    for dq in range(QUADS):
        for far in (0, 1):
            if dq or not far:
                d = spread_vec(mate_z if dq == 0 else lax.rem(2 * quad + 2 * dq, NZ) + far, dq, far)
                d.start()
                sent.append(d)
    lax.fori_loop(9, STEPS - 1, retreat, 0)

    def arrive(r):
        q = lax.rem(quad + r, QUADS)
        ref = quad_rows(q, 0)
        wait = copy(ref, ref, send_z.at[0, 0], recv_z.at[r], dev(dz=mate_z)).wait_recv
        if r:
            wait()
        else:
            pl.when(zb == 0)(wait)
        for kind, to in ((3, across), (2, above), (1, below)):
            go(ref, ref, send_y.at[r, kind], recv_y.at[r, kind], dev(dy=to))
        go(ref, ref, send_c.at[r, 0], recv_c.at[r, 0], dev(dc=sib))

    def arrive_y(r):
        q = lax.rem(quad + r, QUADS)
        for kind in (1, 2, 3):
            ref = quad_rows(q, kind)
            copy(ref, ref, send_y.at[r, kind], recv_y.at[r, kind], dev(dy=above)).wait_recv()
            go(ref, ref, send_c.at[r, kind], recv_c.at[r, kind], dev(dc=sib))

    arrive(0)
    arrive(3)
    arrive(1)
    arrive_y(0)
    arrive(2)
    arrive_y(3)
    arrive_y(1)
    for kind in (1, 2, 3):
        to_mate(kind).wait_recv()
    half_mate = mate.at[pl.ds(base, HALF), :]
    go(half_mate, half_mate, send_m.at[5], recv_m.at[5], dev(dc=sib))
    arrive_y(2)
    for r in range(QUADS):
        for kind in range(4):
            ref = quad_rows(0, 0)
            copy(ref, ref, send_c.at[r, kind], recv_c.at[r, kind], dev(dc=sib)).wait_recv()
    for r in range(QUADS):
        for kind in (0, 1) if r else (zb,):
            v = quad_vec.at[quad, 0]
            copy(v, v, send_v.at[0, 0], recv_v.at[r, kind], dev(dz=mate_z)).wait_recv()
    copy(half_mate, half_mate, send_m.at[5], recv_m.at[5], dev(dc=sib)).wait_recv()

    def chain(way):
        to = dev(dx=lax.rem(x + (NX - 1 if way else 1), NX))
        return copy(chain_out.at[way], ends.at[way], send_d.at[way], recv_d.at[way], to)

    zero = jnp.zeros((1, S), jnp.float32)
    f_row = jnp.where(x == 0, prior_ref[...], zero)
    e_row = zero
    for k in range(QUADS):
        enter_f[k : k + 1, :] = f_row
        f_row = step_on(plane[k], f_row, quad_vec[k, 0])
        n = QUADS - 1 - k
        enter_e[n : n + 1, :] = e_row
        e_row = step_back(plane[n], e_row, quad_vec[n, 1])
    chain_out[0] = jnp.broadcast_to(f_row, (8, S))
    chain_out[1] = jnp.broadcast_to(e_row, (8, S))

    @pl.when(x == 0)
    def _():
        chain(0).start()

    @pl.when(x == NX - 1)
    def _():
        chain(1).start()

    cur[0:S, :] = plane[0]
    ahead[...] = eye

    def compose(k, _):
        @pl.when(k == quad)
        def _():
            ahead[...] = cur[0:S, :]

        cur[0:S, :] = dot3(cur[0:S, :], split(plane[k]))
        return 0

    lax.fori_loop(1, QUADS, compose, 0)

    def pass_on(way):
        chain(way).wait_recv()
        row = ends[way, 0:1, :]
        new = (step_back if way else step_on)(cur[0:S, :], row, chain_out[way, 0:1, :])
        chain_out[way] = jnp.broadcast_to(new, (8, S))
        chain(way).start()

    @pl.when(x == 1)
    def _():
        pass_on(0)

    @pl.when(x == 2)
    def _():
        pass_on(1)

    behind[...] = eye

    @pl.when(quad < QUADS - 1)
    def _():
        behind[...] = plane[lax.rem(quad + 1, QUADS)]

    def compose_after(k, _):
        behind[...] = dot3(behind[...], split(plane[k]))
        return 0

    lax.fori_loop(jnp.minimum(quad + 2, QUADS), QUADS, compose_after, 0)

    @pl.when(x == 1)
    def _():
        pass_on(1)

    @pl.when(x == 2)
    def _():
        pass_on(0)

    @pl.when(x == 0)
    def _():
        chain(1).wait_recv()
        ends[0] = jnp.zeros((8, S), jnp.float32)

    @pl.when(x == NX - 1)
    def _():
        chain(0).wait_recv()
        ends[1] = jnp.zeros((8, S), jnp.float32)

    f_in = step_on(ahead[...], ends[0, 0:1, :], enter_f[pl.ds(quad, 1), :])
    e_in = step_back(behind[...], ends[1, 0:1, :], enter_e[pl.ds(quad, 1), :])
    f_in = jnp.where(zb == 1, step_on(mate[...], f_in, pair_vec[0, 0:1, :]), f_in)
    e_in = jnp.where(zb == 0, step_back(mate[...], e_in, pair_vec[1, 1:2, :]), e_in)
    f_in = jnp.where(c == 1, step_on(pair[0, 0:S, :], f_in, pair[0, S : S + 1, :]), f_in)
    e_in = jnp.where(c == 0, step_back(pair[1, 0:S, :], e_in, pair[1, S + 1 : S + 2, :]), e_in)
    f_col = to_col(f_in)
    e_col = to_col(e_in)
    width = S // NY
    low = lax.rem(y, 2) == 0
    e_last = jnp.where(y < 2, e_in[:, 0:128], e_in[:, 128:])

    def pick(r):
        return jnp.where(low, r[:, 0:width], r[:, width:])

    for t in range(STEPS):
        f = jnp.sum(hist_f[t, 0:S, :] * f_col, axis=0, keepdims=True) + hist_f[t, S : S + 1, :]
        if t < STEPS - 1:
            e = jnp.sum(hist_b[t, 0:S, :] * e_col, axis=0, keepdims=True) + hist_b[t, S : S + 1, :]
        else:
            e = e_last
        out_ref[t : t + 1, :] = pick(f)
        out_ref[STEPS + t : STEPS + t + 1, :] = pick(f + e)

    for d in sent:
        d.wait_send()

    @pl.when(zb == 1)
    def _():
        others(lambda *a: spread(*a).wait_send())

    @pl.when(x < NX - 1)
    def _():
        chain(0).wait_send()

    @pl.when(x > 0)
    def _():
        chain(1).wait_send()


def part_results(both_ref, filt_ref, smooth_ref):
    filt_ref[...] = both_ref[0:STEPS, :]
    smooth_ref[...] = both_ref[STEPS:, :]


def shards(generator, gates, gain_rows, obs_values, obs_rows, obs_counts, prior_mean):
    width = S // NY
    vmem = pl.BlockSpec(memory_space=pltpu.VMEM)
    smem = pl.BlockSpec(memory_space=pltpu.SMEM)
    hbm = pl.BlockSpec(memory_space=pl.ANY)
    f32 = jnp.float32
    dma = pltpu.SemaphoreType.DMA
    inputs = (generator, gates, gain_rows, obs_values, obs_rows)
    both = pl.pallas_call(
        kernel,
        out_shape=jax.ShapeDtypeStruct((2 * STEPS, width), f32),
        in_specs=[hbm] * 5 + [smem, vmem],
        out_specs=vmem,
        scratch_shapes=[pltpu.VMEM(a.shape, a.dtype) for a in inputs]
        + [
            pltpu.VMEM((4, S, S), jnp.bfloat16),
            pltpu.VMEM((STEPS, S), f32),
            pltpu.VMEM((S + 16, S), f32),
            pltpu.VMEM((S, S), f32),
            pltpu.VMEM((STEPS, ROWS, 128), f32),
            pltpu.VMEM((STEPS, ROWS, 128), f32),
            pltpu.VMEM((2, ROWS, S), f32),
            pltpu.VMEM((S, S), f32),
            pltpu.VMEM((S, S), f32),
            pltpu.VMEM((QUADS, S, S), f32),
            pltpu.VMEM((2, 2, S), f32),
            pltpu.VMEM((QUADS, 2, 1, S), f32),
            pltpu.VMEM((2, 8, S), f32),
            pltpu.VMEM((NZ, S), f32),
            pltpu.VMEM((NZ, S), f32),
            pltpu.VMEM((2, 8, S), f32),
            pltpu.VMEM((S, S), f32),
            pltpu.VMEM((S, S), f32),
            dma((5,)),
            dma, dma,
            dma((6,)), dma((6,)),
            dma((4, 2)), dma((4,)),
            dma((4, 4)), dma((4, 4)),
            dma((4, 4)), dma((4, 4)),
            dma((4, 2)), dma((4, 2)),
            dma((2,)), dma((2,)),
        ],
        compiler_params=pltpu.CompilerParams(collective_id=0, has_side_effects=True),
    )(*inputs, obs_counts, prior_mean.reshape(1, S))
    return pl.pallas_call(
        part_results,
        out_shape=[jax.ShapeDtypeStruct((STEPS, width), f32)] * 2,
        in_specs=[vmem],
        out_specs=[vmem] * 2,
    )(both)


def solution(mesh):
    finer = Mesh(mesh.devices.reshape(NX, NZ, NC, NY), TM + ("y",))
    in_specs = (P(), P(TM, None), P(), P(TM, None), P(TM, None), P(TM), P())
    out_specs = (P(TM, "y"), P(TM, "y"))
    return jax.shard_map(shards, mesh=finer, in_specs=in_specs, out_specs=out_specs, check_vma=False)
```

```python
import jax
import jax.numpy as jnp
from jax import lax
from jax.experimental import pallas as pl
from jax.experimental.pallas import tpu as pltpu
from jax.sharding import Mesh
from jax.sharding import PartitionSpec as P

TM = ("x", "z", "c")
NX, NZ, NC, NY = 4, 8, 2, 4
S = 256
STEPS = 16
QUADS = 4
ROWS = S + 8
HALF = S // 2
PART = HALF // 4


def split(x):
    hi = x.astype(jnp.bfloat16)
    return hi, (x - hi.astype(jnp.float32)).astype(jnp.bfloat16)


def mm(a, b):
    return jnp.dot(a, b, preferred_element_type=jnp.float32)


def dot3(a, b):
    ah, al = split(a)
    bh, bl = b
    return mm(ah, bh) + mm(al, bh) + mm(ah, bl)


def eye_mask(rows, columns):
    r = lax.broadcasted_iota(jnp.int32, (rows, columns), 0)
    return r == lax.broadcasted_iota(jnp.int32, (rows, columns), 1)


def to_col(row):
    m = eye_mask(HALF, HALF)
    cols = [jnp.sum(jnp.where(m, row[:, k : k + HALF], 0.0), axis=1, keepdims=True) for k in (0, HALF)]
    return jnp.concatenate(cols, axis=0)


def to_row(col):
    m = eye_mask(HALF, HALF)
    rows = [jnp.sum(jnp.where(m, col[k : k + HALF, :], 0.0), axis=0, keepdims=True) for k in (0, HALF)]
    return jnp.concatenate(rows, axis=1)


def step_on(t, row, add):
    return jnp.sum(t * to_col(row), axis=0, keepdims=True) + add


def step_back(t, row, add):
    return to_row(jnp.sum(t * row, axis=1, keepdims=True)) + add


def kernel(
    gen_hbm, gates_hbm, gain_hbm, vals_hbm, rows_hbm, counts_ref, prior_ref,
    out_ref,
    gen_ref, gates_ref, gain_ref, vals_ref, rows_ref,
    weights, u_s, cur, lines, hist_f, hist_b, pair, slice_vec, own_pair, mate, plane, pair_vec, quad_vec, ends, enter_f, enter_e, chain_out, ahead, behind, total,
    in_sem, send_a, recv_a, send_m, recv_m, send_z, recv_z, send_y, recv_y, send_c, recv_c, send_v, recv_v, send_d, recv_d,
):
    x, z, c, y = (lax.axis_index(a) for a in ("x", "z", "c", "y"))
    sib = 1 - c
    zb = lax.rem(z, 2)
    quad = z // 2
    mate_z = z + 1 - 2 * zb
    above, below, across = (lax.rem(y + k, NY) for k in (1, NY - 1, 2))
    MESH = pl.DeviceIdType.MESH

    def dev(dx=None, dz=None, dc=None, dy=None):
        return tuple(a if d is None else d for a, d in ((x, dx), (z, dz), (c, dc), (y, dy)))

    barrier = pltpu.get_barrier_semaphore()
    partners = [dev(dc=sib), dev(dy=above), dev(dy=below), dev(dy=across)]
    partners += [dev(dz=lax.rem(z + k, NZ)) for k in range(1, NZ)]
    partners += [dev(dx=lax.rem(x + k, NX)) for k in (1, NX - 1)]
    for to in partners:
        pl.semaphore_signal(barrier, inc=1, device_id=to, device_id_type=MESH)

    loads = [
        pltpu.make_async_copy(src, dst, in_sem.at[k])
        for k, (src, dst) in enumerate(
            ((gen_hbm, gen_ref), (rows_hbm, rows_ref), (vals_hbm, vals_ref), (gates_hbm, gates_ref), (gain_hbm, gain_ref))
        )
    ]
    for load in loads:
        load.start()

    loads[0].wait()
    gen = gen_ref[...]
    skew = gen - gen.T
    half_sq = 0.5 * dot3(skew, split(skew))
    eye = jnp.where(eye_mask(S, S), 1.0, 0.0)
    dt = half_sq - skew
    weights[0], weights[1] = split(dt)
    weights[2], weights[3] = split(half_sq + skew)

    lanes = pl.ds(pl.multiple_of((y // 2) * 128, 128), 128)
    loads[3].wait()
    cur[...] = gates_ref[0:1, :] * (eye + dt)
    hist_f[0, 0:S, :] = cur[:, lanes]

    def advance(t, _):
        old = cur[...]
        cur[...] = gates_ref[pl.ds(t, 1), :] * (old + dot3(old, (weights[0], weights[1])))
        hist_f[t, 0:S, :] = cur[:, lanes]
        return 0

    lax.fori_loop(1, STEPS, advance, 0)
    own = pair.at[c]
    own[...] = cur[...]

    pl.semaphore_wait(barrier, len(partners))

    def copy(src, dst, ssem, rsem, to):
        return pltpu.make_async_remote_copy(
            src_ref=src, dst_ref=dst, send_sem=ssem, recv_sem=rsem, device_id=to, device_id_type=MESH
        )

    sent = []

    def go(*args):
        d = copy(*args)
        d.start()
        sent.append(d)

    swap = copy(own, own, send_a, recv_a, dev(dc=sib))
    swap.start()
    sent.append(swap)
    loads[1].wait()
    loads[2].wait()
    slots = vals_ref.shape[1]
    sensors = gain_ref.shape[0]
    lane = lax.broadcasted_iota(jnp.int32, (STEPS, slots), 1)
    line = lax.broadcasted_iota(jnp.int32, (STEPS, slots), 0)
    count = jnp.zeros((STEPS, slots), jnp.int32)
    for t in range(STEPS):
        count = jnp.where(line == t, counts_ref[t], count)
    vals = jnp.where(lane < count, vals_ref[...], 0.0)
    rows = rows_ref[...]
    ids = lax.broadcasted_iota(jnp.int32, (STEPS, sensors), 1)
    w = jnp.zeros((STEPS, sensors), jnp.float32)
    for s in range(slots):
        w = w + jnp.where(rows[:, s : s + 1] == ids, vals[:, s : s + 1], 0.0)
    loads[4].wait()
    u_s[...] = dot3(w, split(gain_ref[...]))

    lines[...] = jnp.zeros((2, 16, S), jnp.float32)

    def affine(k, _):
        g = gates_ref[pl.ds(k, 1), :]
        f = lines[0]
        f = g * (f + dot3(f, (weights[0], weights[1]))) + u_s[pl.ds(k, 1), :]
        lines[0] = f
        hist_f[k, S : S + 8, :] = lines[0, 0:8, lanes]
        t = STEPS - 1 - k
        e = (lines[1] + u_s[pl.ds(t, 1), :]) * gates_ref[pl.ds(t, 1), :]
        lines[1] = e + dot3(e, (weights[2], weights[3]))
        hist_b[lax.rem(t + STEPS - 1, STEPS), S : S + 8, :] = lines[1, 0:8, lanes]
        return 0

    lax.fori_loop(0, 8, affine, 0)
    swap.wait_recv()
    base = pl.multiple_of(c * HALF, HALF)
    own_pair[...] = dot3(pair[0], split(pair[1]))

    kinds = (y, above, below, across)

    def rows_of(kind):
        return pl.ds(pl.multiple_of(c * HALF + kinds[kind] * PART, PART), PART)

    def to_mate(kind):
        return copy(
            own_pair.at[rows_of(kind), :], mate.at[rows_of(kind), :], send_m.at[kind], recv_m.at[kind], dev(dz=mate_z)
        )

    first_rows = to_mate(0)
    first_rows.start()
    sent.append(first_rows)
    lax.fori_loop(8, STEPS, affine, 0)
    slice_vec[c, 0:1, :] = lines[0, 0:1, :]
    slice_vec[c, 1:2, :] = lines[1, 0:1, :]
    swap_slice = copy(slice_vec.at[c], slice_vec.at[c], send_m.at[6], recv_m.at[6], dev(dc=sib))
    swap_slice.start()
    sent.append(swap_slice)

    first_rows.wait_recv()

    def others(act):
        for dq in (2, 1, 3, 0):
            for to_b in (0, 1):
                to = dev(dz=lax.rem(2 * quad + 2 * dq, NZ) + to_b)
                if dq or not to_b:
                    act(to, dq, to_b)

    def quad_rows(q, kind):
        return plane.at[q, rows_of(kind), :]

    def spread(to, dq, to_b):
        ref = quad_rows(quad, 0)
        return copy(ref, ref, send_z.at[dq, to_b], recv_z.at[(4 - dq) % 4], to)

    @pl.when(zb == 1)
    def _():
        plane[quad, rows_of(0), :] = dot3(mate[rows_of(0), :], split(own_pair[...]))
        others(lambda *a: spread(*a).start())

    swap_slice.wait_recv()
    pair_vec[zb, 0:1, :] = step_on(pair[1], slice_vec[0, 0:1, :], slice_vec[1, 0:1, :])
    pair_vec[zb, 1:2, :] = step_back(pair[0], slice_vec[1, 1:2, :], slice_vec[0, 1:2, :])
    swap_vec = copy(pair_vec.at[zb], pair_vec.at[zb], send_m.at[4], recv_m.at[4], dev(dz=mate_z))
    swap_vec.start()
    sent.append(swap_vec)

    for kind in (1, 2, 3):
        d = to_mate(kind)
        d.start()
        sent.append(d)

    def arrive(r):
        q = lax.rem(quad + r, QUADS)
        ref = quad_rows(q, 0)
        wait = copy(ref, ref, send_z.at[0, 0], recv_z.at[r], dev(dz=mate_z)).wait_recv
        if r:
            wait()
        else:
            pl.when(zb == 0)(wait)
        for kind, to in ((3, across), (2, above), (1, below)):
            go(ref, ref, send_y.at[r, kind], recv_y.at[r, kind], dev(dy=to))
        go(ref, ref, send_c.at[r, 0], recv_c.at[r, 0], dev(dc=sib))

    def arrive_y(r):
        q = lax.rem(quad + r, QUADS)
        for kind in (1, 2, 3):
            ref = quad_rows(q, kind)
            copy(ref, ref, send_y.at[r, kind], recv_y.at[r, kind], dev(dy=above)).wait_recv()
            go(ref, ref, send_c.at[r, kind], recv_c.at[r, kind], dev(dc=sib))

    arrive(0)
    arrive(3)

    swap_vec.wait_recv()

    @pl.when(zb == 1)
    def _():
        quad_vec[quad, 0] = step_on(own_pair[...], pair_vec[0, 0:1, :], pair_vec[1, 0:1, :])

    @pl.when(zb == 0)
    def _():
        quad_vec[quad, 1] = step_back(own_pair[...], pair_vec[1, 1:2, :], pair_vec[0, 1:2, :])

    def spread_vec(to_z, dq, far):
        ref = quad_vec.at[quad, 1 - zb]
        return copy(ref, ref, send_v.at[dq, far], recv_v.at[(4 - dq) % 4, 1 - zb], dev(dz=to_z))

    for dq in range(QUADS):
        for far in (0, 1):
            if dq or not far:
                d = spread_vec(mate_z if dq == 0 else lax.rem(2 * quad + 2 * dq, NZ) + far, dq, far)
                d.start()
                sent.append(d)
    arrive(1)
    arrive_y(0)
    arrive(2)
    arrive_y(3)
    arrive_y(1)
    for kind in (1, 2, 3):
        to_mate(kind).wait_recv()
    half_mate = mate.at[pl.ds(base, HALF), :]
    go(half_mate, half_mate, send_m.at[5], recv_m.at[5], dev(dc=sib))
    arrive_y(2)
    for r in range(QUADS):
        for kind in range(4):
            ref = quad_rows(0, 0)
            copy(ref, ref, send_c.at[r, kind], recv_c.at[r, kind], dev(dc=sib)).wait_recv()
    for r in range(QUADS):
        for kind in (0, 1) if r else (zb,):
            v = quad_vec.at[quad, 0]
            copy(v, v, send_v.at[0, 0], recv_v.at[r, kind], dev(dz=mate_z)).wait_recv()
    copy(half_mate, half_mate, send_m.at[5], recv_m.at[5], dev(dc=sib)).wait_recv()

    def chain(way):
        to = dev(dx=lax.rem(x + (NX - 1 if way else 1), NX))
        return copy(chain_out.at[way], ends.at[way], send_d.at[way], recv_d.at[way], to)

    zero = jnp.zeros((1, S), jnp.float32)
    f_row = jnp.where(x == 0, prior_ref[...], zero)
    e_row = zero
    for k in range(QUADS):
        enter_f[k : k + 1, :] = f_row
        f_row = step_on(plane[k], f_row, quad_vec[k, 0])
        n = QUADS - 1 - k
        enter_e[n : n + 1, :] = e_row
        e_row = step_back(plane[n], e_row, quad_vec[n, 1])
    chain_out[0] = jnp.broadcast_to(f_row, (8, S))
    chain_out[1] = jnp.broadcast_to(e_row, (8, S))

    @pl.when(x == 0)
    def _():
        chain(0).start()

    @pl.when(x == NX - 1)
    def _():
        chain(1).start()

    total[...] = plane[0]
    ahead[...] = eye

    def compose(k, _):
        @pl.when(k == quad)
        def _():
            ahead[...] = total[...]

        total[...] = dot3(total[...], split(plane[k]))
        return 0

    lax.fori_loop(1, QUADS, compose, 0)

    def pass_on(way):
        chain(way).wait_recv()
        row = ends[way, 0:1, :]
        new = (step_back if way else step_on)(total[...], row, chain_out[way, 0:1, :])
        chain_out[way] = jnp.broadcast_to(new, (8, S))
        chain(way).start()

    behind[...] = eye

    @pl.when(quad < QUADS - 1)
    def _():
        behind[...] = plane[lax.rem(quad + 1, QUADS)]

    def compose_after(k, _):
        behind[...] = dot3(behind[...], split(plane[k]))
        return 0

    lax.fori_loop(jnp.minimum(quad + 2, QUADS), QUADS, compose_after, 0)

    @pl.when(x == 1)
    def _():
        pass_on(0)

    @pl.when(x == 2)
    def _():
        pass_on(1)

    @pl.when(zb == 1)
    def _():
        ahead[...] = dot3(ahead[...], split(mate[...]))

    @pl.when(c == 1)
    def _():
        ahead[...] = dot3(ahead[...], split(pair[0]))

    @pl.when(zb == 0)
    def _():
        behind[...] = dot3(mate[...], split(behind[...]))

    @pl.when(c == 0)
    def _():
        behind[...] = dot3(pair[1], split(behind[...]))

    f_off = enter_f[pl.ds(quad, 1), :]
    f_off = jnp.where(zb == 1, step_on(mate[...], f_off, pair_vec[0, 0:1, :]), f_off)
    f_off = jnp.where(c == 1, step_on(pair[0], f_off, slice_vec[0, 0:1, :]), f_off)
    e_off = enter_e[pl.ds(quad, 1), :]
    e_off = jnp.where(zb == 0, step_back(mate[...], e_off, pair_vec[1, 1:2, :]), e_off)
    e_off = jnp.where(c == 0, step_back(pair[1], e_off, slice_vec[1, 1:2, :]), e_off)

    cur[...] = eye

    def retreat(k, _):
        t = STEPS - 1 - k
        old = cur[...] * gates_ref[pl.ds(t, 1), :]
        cur[...] = old + dot3(old, (weights[2], weights[3]))
        hist_b[t - 1, 0:S, :] = cur[:, lanes]
        return 0

    lax.fori_loop(0, 5, retreat, 0)

    @pl.when(x == 1)
    def _():
        pass_on(1)

    @pl.when(x == 2)
    def _():
        pass_on(0)

    lax.fori_loop(5, STEPS - 1, retreat, 0)

    @pl.when(x == 0)
    def _():
        chain(1).wait_recv()
        ends[0] = jnp.zeros((8, S), jnp.float32)

    @pl.when(x == NX - 1)
    def _():
        chain(0).wait_recv()
        ends[1] = jnp.zeros((8, S), jnp.float32)

    f_in = step_on(ahead[...], ends[0, 0:1, :], f_off)
    e_in = step_back(behind[...], ends[1, 0:1, :], e_off)
    f_col = to_col(f_in)
    e_col = to_col(e_in)
    width = S // NY
    low = lax.rem(y, 2) == 0
    e_last = jnp.where(y < 2, e_in[:, 0:128], e_in[:, 128:])

    def pick(r):
        return jnp.where(low, r[:, 0:width], r[:, width:])

    for t in range(STEPS):
        f = jnp.sum(hist_f[t, 0:S, :] * f_col, axis=0, keepdims=True) + hist_f[t, S : S + 1, :]
        if t < STEPS - 1:
            e = jnp.sum(hist_b[t, 0:S, :] * e_col, axis=0, keepdims=True) + hist_b[t, S : S + 1, :]
        else:
            e = e_last
        out_ref[t : t + 1, :] = pick(f)
        out_ref[STEPS + t : STEPS + t + 1, :] = pick(f + e)

    for d in sent:
        d.wait_send()

    @pl.when(zb == 1)
    def _():
        others(lambda *a: spread(*a).wait_send())

    @pl.when(x < NX - 1)
    def _():
        chain(0).wait_send()

    @pl.when(x > 0)
    def _():
        chain(1).wait_send()


def part_results(both_ref, filt_ref, smooth_ref):
    filt_ref[...] = both_ref[0:STEPS, :]
    smooth_ref[...] = both_ref[STEPS:, :]


def shards(generator, gates, gain_rows, obs_values, obs_rows, obs_counts, prior_mean):
    width = S // NY
    vmem = pl.BlockSpec(memory_space=pltpu.VMEM)
    smem = pl.BlockSpec(memory_space=pltpu.SMEM)
    hbm = pl.BlockSpec(memory_space=pl.ANY)
    f32 = jnp.float32
    dma = pltpu.SemaphoreType.DMA
    inputs = (generator, gates, gain_rows, obs_values, obs_rows)
    both = pl.pallas_call(
        kernel,
        out_shape=jax.ShapeDtypeStruct((2 * STEPS, width), f32),
        in_specs=[hbm] * 5 + [smem, vmem],
        out_specs=vmem,
        scratch_shapes=[pltpu.VMEM(a.shape, a.dtype) for a in inputs]
        + [
            pltpu.VMEM((4, S, S), jnp.bfloat16),
            pltpu.VMEM((STEPS, S), f32),
            pltpu.VMEM((S, S), f32),
            pltpu.VMEM((2, 16, S), f32),
            pltpu.VMEM((STEPS, ROWS, 128), f32),
            pltpu.VMEM((STEPS, ROWS, 128), f32),
            pltpu.VMEM((2, S, S), f32),
            pltpu.VMEM((2, 2, S), f32),
            pltpu.VMEM((S, S), f32),
            pltpu.VMEM((S, S), f32),
            pltpu.VMEM((QUADS, S, S), f32),
            pltpu.VMEM((2, 2, S), f32),
            pltpu.VMEM((QUADS, 2, 1, S), f32),
            pltpu.VMEM((2, 8, S), f32),
            pltpu.VMEM((NZ, S), f32),
            pltpu.VMEM((NZ, S), f32),
            pltpu.VMEM((2, 8, S), f32),
            pltpu.VMEM((S, S), f32),
            pltpu.VMEM((S, S), f32),
            pltpu.VMEM((S, S), f32),
            dma((5,)),
            dma, dma,
            dma((7,)), dma((7,)),
            dma((4, 2)), dma((4,)),
            dma((4, 4)), dma((4, 4)),
            dma((4, 4)), dma((4, 4)),
            dma((4, 2)), dma((4, 2)),
            dma((2,)), dma((2,)),
        ],
        compiler_params=pltpu.CompilerParams(collective_id=0, has_side_effects=True),
    )(*inputs, obs_counts, prior_mean.reshape(1, S))
    return pl.pallas_call(
        part_results,
        out_shape=[jax.ShapeDtypeStruct((STEPS, width), f32)] * 2,
        in_specs=[vmem],
        out_specs=[vmem] * 2,
    )(both)


def solution(mesh):
    finer = Mesh(mesh.devices.reshape(NX, NZ, NC, NY), TM + ("y",))
    in_specs = (P(), P(TM, None), P(), P(TM, None), P(TM, None), P(TM), P())
    out_specs = (P(TM, "y"), P(TM, "y"))
    return jax.shard_map(shards, mesh=finer, in_specs=in_specs, out_specs=out_specs, check_vma=False)
```

```python
import jax
import jax.numpy as jnp
from jax import lax
from jax.experimental import pallas as pl
from jax.experimental.pallas import tpu as pltpu
from jax.sharding import Mesh
from jax.sharding import PartitionSpec as P

TM = ("x", "z", "c")
NX, NZ, NC, NY = 4, 8, 2, 4
S = 256
STEPS = 16
QUADS = 4
ROWS = S + 8
HALF = S // 2
PART = HALF // 4


def split(x):
    hi = x.astype(jnp.bfloat16)
    return hi, (x - hi.astype(jnp.float32)).astype(jnp.bfloat16)


def mm(a, b):
    return jnp.dot(a, b, preferred_element_type=jnp.float32)


def dot3(a, b):
    ah, al = split(a)
    bh, bl = b
    return mm(ah, bh) + mm(al, bh) + mm(ah, bl)


def eye_mask(rows, columns):
    r = lax.broadcasted_iota(jnp.int32, (rows, columns), 0)
    return r == lax.broadcasted_iota(jnp.int32, (rows, columns), 1)


def to_col(row):
    m = eye_mask(HALF, HALF)
    cols = [jnp.sum(jnp.where(m, row[:, k : k + HALF], 0.0), axis=1, keepdims=True) for k in (0, HALF)]
    return jnp.concatenate(cols, axis=0)


def to_row(col):
    m = eye_mask(HALF, HALF)
    rows = [jnp.sum(jnp.where(m, col[k : k + HALF, :], 0.0), axis=0, keepdims=True) for k in (0, HALF)]
    return jnp.concatenate(rows, axis=1)


def step_on(t, row, add):
    return jnp.sum(t * to_col(row), axis=0, keepdims=True) + add


def step_back(t, row, add):
    return to_row(jnp.sum(t * row, axis=1, keepdims=True)) + add


def kernel(
    gen_hbm, gates_hbm, gain_hbm, vals_hbm, rows_hbm, counts_ref, prior_ref,
    out_ref,
    gen_ref, gates_ref, gain_ref, vals_ref, rows_ref,
    weights, u_s, cur, lines, hist_f, hist_b, pair, slice_vec, lead, own_pair, mate, plane, pair_vec, quad_vec, ends, enter_f, enter_e, chain_out, ahead, behind, total,
    in_sem, send_a, recv_a, send_m, recv_m, send_z, recv_z, send_y, recv_y, send_c, recv_c, send_v, recv_v, send_d, recv_d,
):
    x, z, c, y = (lax.axis_index(a) for a in ("x", "z", "c", "y"))
    sib = 1 - c
    zb = lax.rem(z, 2)
    quad = z // 2
    mate_z = z + 1 - 2 * zb
    above, below, across = (lax.rem(y + k, NY) for k in (1, NY - 1, 2))
    MESH = pl.DeviceIdType.MESH

    def dev(dx=None, dz=None, dc=None, dy=None):
        return tuple(a if d is None else d for a, d in ((x, dx), (z, dz), (c, dc), (y, dy)))

    barrier = pltpu.get_barrier_semaphore()
    partners = [dev(dc=sib), dev(dy=above), dev(dy=below), dev(dy=across)]
    partners += [dev(dz=lax.rem(z + k, NZ)) for k in range(1, NZ)]
    partners += [dev(dx=lax.rem(x + k, NX)) for k in (1, NX - 1)]
    for to in partners:
        pl.semaphore_signal(barrier, inc=1, device_id=to, device_id_type=MESH)

    loads = [
        pltpu.make_async_copy(src, dst, in_sem.at[k])
        for k, (src, dst) in enumerate(
            ((gen_hbm, gen_ref), (rows_hbm, rows_ref), (vals_hbm, vals_ref), (gates_hbm, gates_ref), (gain_hbm, gain_ref))
        )
    ]
    for load in loads:
        load.start()

    loads[0].wait()
    gen = gen_ref[...]
    skew = gen - gen.T
    half_sq = 0.5 * dot3(skew, split(skew))
    eye = jnp.where(eye_mask(S, S), 1.0, 0.0)
    dt = half_sq - skew
    weights[0], weights[1] = split(dt)
    weights[2], weights[3] = split(half_sq + skew)

    lanes = pl.ds(pl.multiple_of((y // 2) * 128, 128), 128)
    loads[3].wait()
    cur[...] = gates_ref[0:1, :] * (eye + dt)
    hist_f[0, 0:S, :] = cur[:, lanes]

    def advance(t, _):
        old = cur[...]
        cur[...] = gates_ref[pl.ds(t, 1), :] * (old + dot3(old, (weights[0], weights[1])))
        hist_f[t, 0:S, :] = cur[:, lanes]
        return 0

    lax.fori_loop(1, STEPS, advance, 0)
    own = pair.at[c]
    own[...] = cur[...]

    pl.semaphore_wait(barrier, len(partners))

    def copy(src, dst, ssem, rsem, to):
        return pltpu.make_async_remote_copy(
            src_ref=src, dst_ref=dst, send_sem=ssem, recv_sem=rsem, device_id=to, device_id_type=MESH
        )

    sent = []

    def go(*args):
        d = copy(*args)
        d.start()
        sent.append(d)

    swap = copy(own, own, send_a, recv_a, dev(dc=sib))
    swap.start()
    sent.append(swap)
    loads[1].wait()
    loads[2].wait()
    slots = vals_ref.shape[1]
    sensors = gain_ref.shape[0]
    lane = lax.broadcasted_iota(jnp.int32, (STEPS, slots), 1)
    line = lax.broadcasted_iota(jnp.int32, (STEPS, slots), 0)
    count = jnp.zeros((STEPS, slots), jnp.int32)
    for t in range(STEPS):
        count = jnp.where(line == t, counts_ref[t], count)
    vals = jnp.where(lane < count, vals_ref[...], 0.0)
    rows = rows_ref[...]
    ids = lax.broadcasted_iota(jnp.int32, (STEPS, sensors), 1)
    w = jnp.zeros((STEPS, sensors), jnp.float32)
    for s in range(slots):
        w = w + jnp.where(rows[:, s : s + 1] == ids, vals[:, s : s + 1], 0.0)
    loads[4].wait()
    u_s[...] = dot3(w, split(gain_ref[...]))

    lines[...] = jnp.zeros((2, 16, S), jnp.float32)

    def affine(k, _):
        g = gates_ref[pl.ds(k, 1), :]
        f = lines[0]
        f = g * (f + dot3(f, (weights[0], weights[1]))) + u_s[pl.ds(k, 1), :]
        lines[0] = f
        hist_f[k, S : S + 8, :] = lines[0, 0:8, lanes]
        t = STEPS - 1 - k
        e = (lines[1] + u_s[pl.ds(t, 1), :]) * gates_ref[pl.ds(t, 1), :]
        lines[1] = e + dot3(e, (weights[2], weights[3]))
        hist_b[lax.rem(t + STEPS - 1, STEPS), S : S + 8, :] = lines[1, 0:8, lanes]
        return 0

    lax.fori_loop(0, 4, affine, 0)
    swap.wait_recv()
    base = pl.multiple_of(c * HALF, HALF)

    kinds = (y, above, below, across)

    def rows_of(kind):
        return pl.ds(pl.multiple_of(c * HALF + kinds[kind] * PART, PART), PART)

    def to_mate(kind):
        return copy(
            own_pair.at[rows_of(kind), :], mate.at[rows_of(kind), :], send_m.at[kind], recv_m.at[kind], dev(dz=mate_z)
        )

    lead[...] = dot3(pair[0, rows_of(0), :], split(pair[1]))
    first_rows = copy(lead, mate.at[rows_of(0), :], send_m.at[0], recv_m.at[0], dev(dz=mate_z))
    first_rows.start()
    sent.append(first_rows)
    own_pair[...] = dot3(pair[0], split(pair[1]))
    lax.fori_loop(4, 10, affine, 0)

    first_rows.wait_recv()

    def others(act):
        for dq, to_b in ((0, 0), (1, 0), (3, 1), (1, 1), (3, 0), (2, 0), (2, 1)):
            act(dev(dz=lax.rem(2 * quad + 2 * dq, NZ) + to_b), dq, to_b)

    def quad_rows(q, kind):
        return plane.at[q, rows_of(kind), :]

    def spread(to, dq, to_b):
        ref = quad_rows(quad, 0)
        return copy(ref, ref, send_z.at[dq, to_b], recv_z.at[(4 - dq) % 4], to)

    @pl.when(zb == 1)
    def _():
        plane[quad, rows_of(0), :] = dot3(mate[rows_of(0), :], split(own_pair[...]))
        others(lambda *a: spread(*a).start())

    lax.fori_loop(10, STEPS, affine, 0)
    slice_vec[c, 0:1, :] = lines[0, 0:1, :]
    slice_vec[c, 1:2, :] = lines[1, 0:1, :]
    swap_slice = copy(slice_vec.at[c], slice_vec.at[c], send_m.at[6], recv_m.at[6], dev(dc=sib))
    swap_slice.start()
    sent.append(swap_slice)

    swap_slice.wait_recv()
    pair_vec[zb, 0:1, :] = step_on(pair[1], slice_vec[0, 0:1, :], slice_vec[1, 0:1, :])
    pair_vec[zb, 1:2, :] = step_back(pair[0], slice_vec[1, 1:2, :], slice_vec[0, 1:2, :])
    swap_vec = copy(pair_vec.at[zb], pair_vec.at[zb], send_m.at[4], recv_m.at[4], dev(dz=mate_z))
    swap_vec.start()
    sent.append(swap_vec)

    for kind in (1, 2, 3):
        d = to_mate(kind)
        d.start()
        sent.append(d)

    def arrive(r):
        q = lax.rem(quad + r, QUADS)
        ref = quad_rows(q, 0)
        wait = copy(ref, ref, send_z.at[0, 0], recv_z.at[r], dev(dz=mate_z)).wait_recv
        if r:
            wait()
        else:
            pl.when(zb == 0)(wait)
        for kind, to in ((3, across), (2, above), (1, below)):
            go(ref, ref, send_y.at[r, kind], recv_y.at[r, kind], dev(dy=to))
        go(ref, ref, send_c.at[r, 0], recv_c.at[r, 0], dev(dc=sib))

    def arrive_y(r):
        q = lax.rem(quad + r, QUADS)
        for kind in (1, 2, 3):
            ref = quad_rows(q, kind)
            copy(ref, ref, send_y.at[r, kind], recv_y.at[r, kind], dev(dy=above)).wait_recv()
            go(ref, ref, send_c.at[r, kind], recv_c.at[r, kind], dev(dc=sib))

    arrive(0)
    arrive(3)

    swap_vec.wait_recv()

    @pl.when(zb == 1)
    def _():
        quad_vec[quad, 0] = step_on(own_pair[...], pair_vec[0, 0:1, :], pair_vec[1, 0:1, :])

    @pl.when(zb == 0)
    def _():
        quad_vec[quad, 1] = step_back(own_pair[...], pair_vec[1, 1:2, :], pair_vec[0, 1:2, :])

    def spread_vec(to_z, dq, far):
        ref = quad_vec.at[quad, 1 - zb]
        return copy(ref, ref, send_v.at[dq, far], recv_v.at[(4 - dq) % 4, 1 - zb], dev(dz=to_z))

    for dq in range(QUADS):
        for far in (0, 1):
            if dq or not far:
                d = spread_vec(mate_z if dq == 0 else lax.rem(2 * quad + 2 * dq, NZ) + far, dq, far)
                d.start()
                sent.append(d)
    arrive(1)
    arrive_y(0)
    arrive(2)
    arrive_y(3)
    arrive_y(1)
    for kind in (1, 2, 3):
        to_mate(kind).wait_recv()
    half_mate = mate.at[pl.ds(base, HALF), :]
    go(half_mate, half_mate, send_m.at[5], recv_m.at[5], dev(dc=sib))
    arrive_y(2)
    for r in range(QUADS):
        for kind in range(4):
            ref = quad_rows(0, 0)
            copy(ref, ref, send_c.at[r, kind], recv_c.at[r, kind], dev(dc=sib)).wait_recv()
    for r in range(QUADS):
        for kind in (0, 1) if r else (zb,):
            v = quad_vec.at[quad, 0]
            copy(v, v, send_v.at[0, 0], recv_v.at[r, kind], dev(dz=mate_z)).wait_recv()
    copy(half_mate, half_mate, send_m.at[5], recv_m.at[5], dev(dc=sib)).wait_recv()

    def chain(way):
        to = dev(dx=lax.rem(x + (NX - 1 if way else 1), NX))
        return copy(chain_out.at[way], ends.at[way], send_d.at[way], recv_d.at[way], to)

    zero = jnp.zeros((1, S), jnp.float32)
    f_row = jnp.where(x == 0, prior_ref[...], zero)
    e_row = zero
    for k in range(QUADS):
        enter_f[k : k + 1, :] = f_row
        f_row = step_on(plane[k], f_row, quad_vec[k, 0])
        n = QUADS - 1 - k
        enter_e[n : n + 1, :] = e_row
        e_row = step_back(plane[n], e_row, quad_vec[n, 1])
    chain_out[0] = jnp.broadcast_to(f_row, (8, S))
    chain_out[1] = jnp.broadcast_to(e_row, (8, S))

    @pl.when(x == 0)
    def _():
        chain(0).start()

    @pl.when(x == NX - 1)
    def _():
        chain(1).start()

    total[...] = plane[0]
    ahead[...] = eye

    def compose(k, _):
        @pl.when(k == quad)
        def _():
            ahead[...] = total[...]

        total[...] = dot3(total[...], split(plane[k]))
        return 0

    lax.fori_loop(1, QUADS, compose, 0)

    def pass_on(way):
        chain(way).wait_recv()
        row = ends[way, 0:1, :]
        new = (step_back if way else step_on)(total[...], row, chain_out[way, 0:1, :])
        chain_out[way] = jnp.broadcast_to(new, (8, S))
        chain(way).start()

    behind[...] = eye

    @pl.when(quad < QUADS - 1)
    def _():
        behind[...] = plane[lax.rem(quad + 1, QUADS)]

    def compose_after(k, _):
        behind[...] = dot3(behind[...], split(plane[k]))
        return 0

    lax.fori_loop(jnp.minimum(quad + 2, QUADS), QUADS, compose_after, 0)

    @pl.when(x == 1)
    def _():
        pass_on(0)

    @pl.when(x == 2)
    def _():
        pass_on(1)

    @pl.when(zb == 1)
    def _():
        ahead[...] = dot3(ahead[...], split(mate[...]))

    @pl.when(c == 1)
    def _():
        ahead[...] = dot3(ahead[...], split(pair[0]))

    @pl.when(zb == 0)
    def _():
        behind[...] = dot3(mate[...], split(behind[...]))

    @pl.when(c == 0)
    def _():
        behind[...] = dot3(pair[1], split(behind[...]))

    f_off = enter_f[pl.ds(quad, 1), :]
    f_off = jnp.where(zb == 1, step_on(mate[...], f_off, pair_vec[0, 0:1, :]), f_off)
    f_off = jnp.where(c == 1, step_on(pair[0], f_off, slice_vec[0, 0:1, :]), f_off)
    e_off = enter_e[pl.ds(quad, 1), :]
    e_off = jnp.where(zb == 0, step_back(mate[...], e_off, pair_vec[1, 1:2, :]), e_off)
    e_off = jnp.where(c == 0, step_back(pair[1], e_off, slice_vec[1, 1:2, :]), e_off)

    cur[...] = eye

    def retreat(k, _):
        t = STEPS - 1 - k
        old = cur[...] * gates_ref[pl.ds(t, 1), :]
        cur[...] = old + dot3(old, (weights[2], weights[3]))
        hist_b[t - 1, 0:S, :] = cur[:, lanes]
        return 0

    lax.fori_loop(0, 5, retreat, 0)

    @pl.when(x == 1)
    def _():
        pass_on(1)

    @pl.when(x == 2)
    def _():
        pass_on(0)

    lax.fori_loop(5, STEPS - 1, retreat, 0)

    @pl.when(x == 0)
    def _():
        chain(1).wait_recv()
        ends[0] = jnp.zeros((8, S), jnp.float32)

    @pl.when(x == NX - 1)
    def _():
        chain(0).wait_recv()
        ends[1] = jnp.zeros((8, S), jnp.float32)

    f_in = step_on(ahead[...], ends[0, 0:1, :], f_off)
    e_in = step_back(behind[...], ends[1, 0:1, :], e_off)
    f_col = to_col(f_in)
    e_col = to_col(e_in)
    width = S // NY
    low = lax.rem(y, 2) == 0
    e_last = jnp.where(y < 2, e_in[:, 0:128], e_in[:, 128:])

    def pick(r):
        return jnp.where(low, r[:, 0:width], r[:, width:])

    for t in range(STEPS):
        f = jnp.sum(hist_f[t, 0:S, :] * f_col, axis=0, keepdims=True) + hist_f[t, S : S + 1, :]
        if t < STEPS - 1:
            e = jnp.sum(hist_b[t, 0:S, :] * e_col, axis=0, keepdims=True) + hist_b[t, S : S + 1, :]
        else:
            e = e_last
        out_ref[t : t + 1, :] = pick(f)
        out_ref[STEPS + t : STEPS + t + 1, :] = pick(f + e)

    for d in sent:
        d.wait_send()

    @pl.when(zb == 1)
    def _():
        others(lambda *a: spread(*a).wait_send())

    @pl.when(x < NX - 1)
    def _():
        chain(0).wait_send()

    @pl.when(x > 0)
    def _():
        chain(1).wait_send()


def part_results(both_ref, filt_ref, smooth_ref):
    filt_ref[...] = both_ref[0:STEPS, :]
    smooth_ref[...] = both_ref[STEPS:, :]


def shards(generator, gates, gain_rows, obs_values, obs_rows, obs_counts, prior_mean):
    width = S // NY
    vmem = pl.BlockSpec(memory_space=pltpu.VMEM)
    smem = pl.BlockSpec(memory_space=pltpu.SMEM)
    hbm = pl.BlockSpec(memory_space=pl.ANY)
    f32 = jnp.float32
    dma = pltpu.SemaphoreType.DMA
    inputs = (generator, gates, gain_rows, obs_values, obs_rows)
    both = pl.pallas_call(
        kernel,
        out_shape=jax.ShapeDtypeStruct((2 * STEPS, width), f32),
        in_specs=[hbm] * 5 + [smem, vmem],
        out_specs=vmem,
        scratch_shapes=[pltpu.VMEM(a.shape, a.dtype) for a in inputs]
        + [
            pltpu.VMEM((4, S, S), jnp.bfloat16),
            pltpu.VMEM((STEPS, S), f32),
            pltpu.VMEM((S, S), f32),
            pltpu.VMEM((2, 16, S), f32),
            pltpu.VMEM((STEPS, ROWS, 128), f32),
            pltpu.VMEM((STEPS, ROWS, 128), f32),
            pltpu.VMEM((2, S, S), f32),
            pltpu.VMEM((2, 2, S), f32),
            pltpu.VMEM((PART, S), f32),
            pltpu.VMEM((S, S), f32),
            pltpu.VMEM((S, S), f32),
            pltpu.VMEM((QUADS, S, S), f32),
            pltpu.VMEM((2, 2, S), f32),
            pltpu.VMEM((QUADS, 2, 1, S), f32),
            pltpu.VMEM((2, 8, S), f32),
            pltpu.VMEM((NZ, S), f32),
            pltpu.VMEM((NZ, S), f32),
            pltpu.VMEM((2, 8, S), f32),
            pltpu.VMEM((S, S), f32),
            pltpu.VMEM((S, S), f32),
            pltpu.VMEM((S, S), f32),
            dma((5,)),
            dma, dma,
            dma((7,)), dma((7,)),
            dma((4, 2)), dma((4,)),
            dma((4, 4)), dma((4, 4)),
            dma((4, 4)), dma((4, 4)),
            dma((4, 2)), dma((4, 2)),
            dma((2,)), dma((2,)),
        ],
        compiler_params=pltpu.CompilerParams(collective_id=0, has_side_effects=True),
    )(*inputs, obs_counts, prior_mean.reshape(1, S))
    return pl.pallas_call(
        part_results,
        out_shape=[jax.ShapeDtypeStruct((STEPS, width), f32)] * 2,
        in_specs=[vmem],
        out_specs=[vmem] * 2,
    )(both)


def solution(mesh):
    finer = Mesh(mesh.devices.reshape(NX, NZ, NC, NY), TM + ("y",))
    in_specs = (P(), P(TM, None), P(), P(TM, None), P(TM, None), P(TM), P())
    out_specs = (P(TM, "y"), P(TM, "y"))
    return jax.shard_map(shards, mesh=finer, in_specs=in_specs, out_specs=out_specs, check_vma=False)
```

```python
import jax
import jax.numpy as jnp
from jax import lax
from jax.experimental import pallas as pl
from jax.experimental.pallas import tpu as pltpu
from jax.sharding import Mesh
from jax.sharding import PartitionSpec as P

TM = ("x", "z", "c")
NX, NZ, NC, NY = 4, 8, 2, 4
S = 256
STEPS = 16
QUADS = 4
ROWS = S + 8
HALF = S // 2
PART = HALF // 4


def split(x):
    hi = x.astype(jnp.bfloat16)
    return hi, (x - hi.astype(jnp.float32)).astype(jnp.bfloat16)


def mm(a, b):
    return jnp.dot(a, b, preferred_element_type=jnp.float32)


def dot3(a, b):
    ah, al = split(a)
    bh, bl = b
    return mm(ah, bh) + mm(al, bh) + mm(ah, bl)


def eye_mask(rows, columns):
    r = lax.broadcasted_iota(jnp.int32, (rows, columns), 0)
    return r == lax.broadcasted_iota(jnp.int32, (rows, columns), 1)


def to_col(row):
    m = eye_mask(HALF, HALF)
    cols = [jnp.sum(jnp.where(m, row[:, k : k + HALF], 0.0), axis=1, keepdims=True) for k in (0, HALF)]
    return jnp.concatenate(cols, axis=0)


def to_row(col):
    m = eye_mask(HALF, HALF)
    rows = [jnp.sum(jnp.where(m, col[k : k + HALF, :], 0.0), axis=0, keepdims=True) for k in (0, HALF)]
    return jnp.concatenate(rows, axis=1)


def step_on(t, row, add):
    return jnp.sum(t * to_col(row), axis=0, keepdims=True) + add


def step_back(t, row, add):
    return to_row(jnp.sum(t * row, axis=1, keepdims=True)) + add


def kernel(
    gen_hbm, gates_hbm, gain_hbm, vals_hbm, rows_hbm, counts_ref, prior_ref,
    out_ref,
    gen_ref, gates_ref, gain_ref, vals_ref, rows_ref,
    weights, u_s, cur, lines, hist_f, hist_b, pair, slice_vec, lead, lead_in, own_pair, mate, plane, pair_vec, quad_vec, ends, enter_f, enter_e, chain_out, ahead, behind, total,
    in_sem, send_a, recv_a, send_m, recv_m, send_z, recv_z, send_y, recv_y, send_c, recv_c, send_v, recv_v, send_d, recv_d,
):
    x, z, c, y = (lax.axis_index(a) for a in ("x", "z", "c", "y"))
    sib = 1 - c
    zb = lax.rem(z, 2)
    quad = z // 2
    mate_z = z + 1 - 2 * zb
    above, below, across = (lax.rem(y + k, NY) for k in (1, NY - 1, 2))
    MESH = pl.DeviceIdType.MESH

    def dev(dx=None, dz=None, dc=None, dy=None):
        return tuple(a if d is None else d for a, d in ((x, dx), (z, dz), (c, dc), (y, dy)))

    barrier = pltpu.get_barrier_semaphore()
    partners = [dev(dc=sib), dev(dy=above), dev(dy=below), dev(dy=across)]
    partners += [dev(dz=lax.rem(z + k, NZ)) for k in range(1, NZ)]
    partners += [dev(dz=lax.rem(z + k, NZ), dc=sib) for k in range(1, NZ)]
    partners += [dev(dx=lax.rem(x + k, NX)) for k in (1, NX - 1)]
    for to in partners:
        pl.semaphore_signal(barrier, inc=1, device_id=to, device_id_type=MESH)

    loads = [
        pltpu.make_async_copy(src, dst, in_sem.at[k])
        for k, (src, dst) in enumerate(
            ((gen_hbm, gen_ref), (rows_hbm, rows_ref), (vals_hbm, vals_ref), (gates_hbm, gates_ref), (gain_hbm, gain_ref))
        )
    ]
    for load in loads:
        load.start()

    loads[0].wait()
    gen = gen_ref[...]
    skew = gen - gen.T
    half_sq = 0.5 * dot3(skew, split(skew))
    eye = jnp.where(eye_mask(S, S), 1.0, 0.0)
    dt = half_sq - skew
    weights[0], weights[1] = split(dt)
    weights[2], weights[3] = split(half_sq + skew)

    lanes = pl.ds(pl.multiple_of((y // 2) * 128, 128), 128)
    loads[3].wait()
    cur[...] = gates_ref[0:1, :] * (eye + dt)
    hist_f[0, 0:S, :] = cur[:, lanes]

    def advance(t, _):
        old = cur[...]
        cur[...] = gates_ref[pl.ds(t, 1), :] * (old + dot3(old, (weights[0], weights[1])))
        hist_f[t, 0:S, :] = cur[:, lanes]
        return 0

    lax.fori_loop(1, STEPS, advance, 0)
    own = pair.at[c]
    own[...] = cur[...]

    pl.semaphore_wait(barrier, len(partners))

    def copy(src, dst, ssem, rsem, to):
        return pltpu.make_async_remote_copy(
            src_ref=src, dst_ref=dst, send_sem=ssem, recv_sem=rsem, device_id=to, device_id_type=MESH
        )

    sent = []

    def go(*args):
        d = copy(*args)
        d.start()
        sent.append(d)

    pos = zb * 2 + c

    def block_at(k):
        return pl.ds(pl.multiple_of(k * HALF + y * PART, PART), PART)

    to_next = copy(
        lead, lead_in, send_m.at[7], recv_m.at[7],
        dev(dz=jnp.where(c == 1, mate_z, z), dc=sib),
    )

    @pl.when(pos == 0)
    def _():
        for k in (0, 1):
            lead[k * PART : (k + 1) * PART, :] = cur[block_at(k), :]
        to_next.start()

    swap = copy(own, own, send_a, recv_a, dev(dc=sib))
    swap.start()
    sent.append(swap)

    def multiply():
        to_next.wait_recv()
        lead[...] = dot3(lead_in[...], split(cur[...]))

    @pl.when(pos == 1)
    def _():
        multiply()
        to_next.start()

    loads[1].wait()
    loads[2].wait()
    slots = vals_ref.shape[1]
    sensors = gain_ref.shape[0]
    lane = lax.broadcasted_iota(jnp.int32, (STEPS, slots), 1)
    line = lax.broadcasted_iota(jnp.int32, (STEPS, slots), 0)
    count = jnp.zeros((STEPS, slots), jnp.int32)
    for t in range(STEPS):
        count = jnp.where(line == t, counts_ref[t], count)
    vals = jnp.where(lane < count, vals_ref[...], 0.0)
    rows = rows_ref[...]
    ids = lax.broadcasted_iota(jnp.int32, (STEPS, sensors), 1)
    w = jnp.zeros((STEPS, sensors), jnp.float32)
    for s in range(slots):
        w = w + jnp.where(rows[:, s : s + 1] == ids, vals[:, s : s + 1], 0.0)
    loads[4].wait()
    u_s[...] = dot3(w, split(gain_ref[...]))

    lines[...] = jnp.zeros((2, 16, S), jnp.float32)

    def affine(k, _):
        g = gates_ref[pl.ds(k, 1), :]
        f = lines[0]
        f = g * (f + dot3(f, (weights[0], weights[1]))) + u_s[pl.ds(k, 1), :]
        lines[0] = f
        hist_f[k, S : S + 8, :] = lines[0, 0:8, lanes]
        t = STEPS - 1 - k
        e = (lines[1] + u_s[pl.ds(t, 1), :]) * gates_ref[pl.ds(t, 1), :]
        lines[1] = e + dot3(e, (weights[2], weights[3]))
        hist_b[lax.rem(t + STEPS - 1, STEPS), S : S + 8, :] = lines[1, 0:8, lanes]
        return 0

    lax.fori_loop(0, 7, affine, 0)

    @pl.when(pos == 2)
    def _():
        multiply()
        to_next.start()

    lax.fori_loop(7, 10, affine, 0)
    base = pl.multiple_of(c * HALF, HALF)

    kinds = (y, above, below, across)

    def rows_of(kind):
        return pl.ds(pl.multiple_of(c * HALF + kinds[kind] * PART, PART), PART)

    def to_mate(kind):
        return copy(
            own_pair.at[rows_of(kind), :], mate.at[rows_of(kind), :], send_m.at[kind], recv_m.at[kind], dev(dz=mate_z)
        )

    def others(act):
        for dq, to_b in ((0, 1), (0, 0), (1, 0), (3, 1), (1, 1), (3, 0), (2, 0), (2, 1)):
            for k in (0, 1):
                if dq or not to_b or not k:
                    act(dq, to_b, k)

    def quad_rows(q, kind):
        return plane.at[q, rows_of(kind), :]

    def spread(dq, to_b, k):
        return copy(
            lead.at[pl.ds(k * PART, PART), :], plane.at[quad, block_at(k), :],
            send_z.at[dq, to_b, k], recv_z.at[(4 - dq) % 4], dev(dz=lax.rem(2 * quad + 2 * dq, NZ) + to_b, dc=k),
        )

    @pl.when(pos == 3)
    def _():
        multiply()
        others(lambda *a: spread(*a).start())
        plane[quad, block_at(1), :] = lead[PART:, :]

    swap.wait_recv()
    own_pair[...] = dot3(pair[0], split(pair[1]))

    lax.fori_loop(10, STEPS, affine, 0)
    slice_vec[c, 0:1, :] = lines[0, 0:1, :]
    slice_vec[c, 1:2, :] = lines[1, 0:1, :]
    swap_slice = copy(slice_vec.at[c], slice_vec.at[c], send_m.at[6], recv_m.at[6], dev(dc=sib))
    swap_slice.start()
    sent.append(swap_slice)

    swap_slice.wait_recv()
    pair_vec[zb, 0:1, :] = step_on(pair[1], slice_vec[0, 0:1, :], slice_vec[1, 0:1, :])
    pair_vec[zb, 1:2, :] = step_back(pair[0], slice_vec[1, 1:2, :], slice_vec[0, 1:2, :])
    swap_vec = copy(pair_vec.at[zb], pair_vec.at[zb], send_m.at[4], recv_m.at[4], dev(dz=mate_z))
    swap_vec.start()
    sent.append(swap_vec)

    for kind in range(4):
        d = to_mate(kind)
        d.start()
        sent.append(d)

    def arrive(r):
        q = lax.rem(quad + r, QUADS)
        ref = quad_rows(q, 0)
        wait = copy(ref, ref, send_z.at[0, 0, 0], recv_z.at[r], dev(dz=mate_z)).wait_recv
        if r:
            wait()
        else:
            pl.when(pos < 3)(wait)
        for kind, to in ((3, across), (2, above), (1, below)):
            go(ref, ref, send_y.at[r, kind], recv_y.at[r, kind], dev(dy=to))
        go(ref, ref, send_c.at[r, 0], recv_c.at[r, 0], dev(dc=sib))

    def arrive_y(r):
        q = lax.rem(quad + r, QUADS)
        for kind in (1, 2, 3):
            ref = quad_rows(q, kind)
            copy(ref, ref, send_y.at[r, kind], recv_y.at[r, kind], dev(dy=above)).wait_recv()
            go(ref, ref, send_c.at[r, kind], recv_c.at[r, kind], dev(dc=sib))

    arrive(0)
    arrive(3)

    swap_vec.wait_recv()

    @pl.when(zb == 1)
    def _():
        quad_vec[quad, 0] = step_on(own_pair[...], pair_vec[0, 0:1, :], pair_vec[1, 0:1, :])

    @pl.when(zb == 0)
    def _():
        quad_vec[quad, 1] = step_back(own_pair[...], pair_vec[1, 1:2, :], pair_vec[0, 1:2, :])

    def spread_vec(to_z, dq, far):
        ref = quad_vec.at[quad, 1 - zb]
        return copy(ref, ref, send_v.at[dq, far], recv_v.at[(4 - dq) % 4, 1 - zb], dev(dz=to_z))

    for dq in range(QUADS):
        for far in (0, 1):
            if dq or not far:
                d = spread_vec(mate_z if dq == 0 else lax.rem(2 * quad + 2 * dq, NZ) + far, dq, far)
                d.start()
                sent.append(d)
    arrive(1)
    arrive_y(0)
    arrive(2)
    arrive_y(3)
    arrive_y(1)
    for kind in range(4):
        to_mate(kind).wait_recv()
    half_mate = mate.at[pl.ds(base, HALF), :]
    go(half_mate, half_mate, send_m.at[5], recv_m.at[5], dev(dc=sib))
    arrive_y(2)
    for r in range(QUADS):
        for kind in range(4):
            ref = quad_rows(0, 0)
            copy(ref, ref, send_c.at[r, kind], recv_c.at[r, kind], dev(dc=sib)).wait_recv()
    for r in range(QUADS):
        for kind in (0, 1) if r else (zb,):
            v = quad_vec.at[quad, 0]
            copy(v, v, send_v.at[0, 0], recv_v.at[r, kind], dev(dz=mate_z)).wait_recv()
    copy(half_mate, half_mate, send_m.at[5], recv_m.at[5], dev(dc=sib)).wait_recv()

    def chain(way):
        to = dev(dx=lax.rem(x + (NX - 1 if way else 1), NX))
        return copy(chain_out.at[way], ends.at[way], send_d.at[way], recv_d.at[way], to)

    zero = jnp.zeros((1, S), jnp.float32)
    f_row = jnp.where(x == 0, prior_ref[...], zero)
    e_row = zero
    for k in range(QUADS):
        enter_f[k : k + 1, :] = f_row
        f_row = step_on(plane[k], f_row, quad_vec[k, 0])
        n = QUADS - 1 - k
        enter_e[n : n + 1, :] = e_row
        e_row = step_back(plane[n], e_row, quad_vec[n, 1])
    chain_out[0] = jnp.broadcast_to(f_row, (8, S))
    chain_out[1] = jnp.broadcast_to(e_row, (8, S))

    @pl.when(x == 0)
    def _():
        chain(0).start()

    @pl.when(x == NX - 1)
    def _():
        chain(1).start()

    total[...] = plane[0]
    ahead[...] = eye

    def compose(k, _):
        @pl.when(k == quad)
        def _():
            ahead[...] = total[...]

        total[...] = dot3(total[...], split(plane[k]))
        return 0

    lax.fori_loop(1, QUADS, compose, 0)

    def pass_on(way):
        chain(way).wait_recv()
        row = ends[way, 0:1, :]
        new = (step_back if way else step_on)(total[...], row, chain_out[way, 0:1, :])
        chain_out[way] = jnp.broadcast_to(new, (8, S))
        chain(way).start()

    behind[...] = eye

    @pl.when(quad < QUADS - 1)
    def _():
        behind[...] = plane[lax.rem(quad + 1, QUADS)]

    def compose_after(k, _):
        behind[...] = dot3(behind[...], split(plane[k]))
        return 0

    lax.fori_loop(jnp.minimum(quad + 2, QUADS), QUADS, compose_after, 0)

    @pl.when(x == 1)
    def _():
        pass_on(0)

    @pl.when(x == 2)
    def _():
        pass_on(1)

    @pl.when(zb == 1)
    def _():
        ahead[...] = dot3(ahead[...], split(mate[...]))

    @pl.when(c == 1)
    def _():
        ahead[...] = dot3(ahead[...], split(pair[0]))

    @pl.when(zb == 0)
    def _():
        behind[...] = dot3(mate[...], split(behind[...]))

    @pl.when(c == 0)
    def _():
        behind[...] = dot3(pair[1], split(behind[...]))

    f_off = enter_f[pl.ds(quad, 1), :]
    f_off = jnp.where(zb == 1, step_on(mate[...], f_off, pair_vec[0, 0:1, :]), f_off)
    f_off = jnp.where(c == 1, step_on(pair[0], f_off, slice_vec[0, 0:1, :]), f_off)
    e_off = enter_e[pl.ds(quad, 1), :]
    e_off = jnp.where(zb == 0, step_back(mate[...], e_off, pair_vec[1, 1:2, :]), e_off)
    e_off = jnp.where(c == 0, step_back(pair[1], e_off, slice_vec[1, 1:2, :]), e_off)

    cur[...] = eye

    def retreat(k, _):
        t = STEPS - 1 - k
        old = cur[...] * gates_ref[pl.ds(t, 1), :]
        cur[...] = old + dot3(old, (weights[2], weights[3]))
        hist_b[t - 1, 0:S, :] = cur[:, lanes]
        return 0

    lax.fori_loop(0, 5, retreat, 0)

    @pl.when(x == 1)
    def _():
        pass_on(1)

    @pl.when(x == 2)
    def _():
        pass_on(0)

    lax.fori_loop(5, STEPS - 1, retreat, 0)

    @pl.when(x == 0)
    def _():
        chain(1).wait_recv()
        ends[0] = jnp.zeros((8, S), jnp.float32)

    @pl.when(x == NX - 1)
    def _():
        chain(0).wait_recv()
        ends[1] = jnp.zeros((8, S), jnp.float32)

    f_in = step_on(ahead[...], ends[0, 0:1, :], f_off)
    e_in = step_back(behind[...], ends[1, 0:1, :], e_off)
    f_col = to_col(f_in)
    e_col = to_col(e_in)
    width = S // NY
    low = lax.rem(y, 2) == 0
    e_last = jnp.where(y < 2, e_in[:, 0:128], e_in[:, 128:])

    def pick(r):
        return jnp.where(low, r[:, 0:width], r[:, width:])

    for t in range(STEPS):
        f = jnp.sum(hist_f[t, 0:S, :] * f_col, axis=0, keepdims=True) + hist_f[t, S : S + 1, :]
        if t < STEPS - 1:
            e = jnp.sum(hist_b[t, 0:S, :] * e_col, axis=0, keepdims=True) + hist_b[t, S : S + 1, :]
        else:
            e = e_last
        out_ref[t : t + 1, :] = pick(f)
        out_ref[STEPS + t : STEPS + t + 1, :] = pick(f + e)

    for d in sent:
        d.wait_send()

    @pl.when(pos < 3)
    def _():
        to_next.wait_send()

    @pl.when(pos == 3)
    def _():
        others(lambda *a: spread(*a).wait_send())

    @pl.when(x < NX - 1)
    def _():
        chain(0).wait_send()

    @pl.when(x > 0)
    def _():
        chain(1).wait_send()


def part_results(both_ref, filt_ref, smooth_ref):
    filt_ref[...] = both_ref[0:STEPS, :]
    smooth_ref[...] = both_ref[STEPS:, :]


def shards(generator, gates, gain_rows, obs_values, obs_rows, obs_counts, prior_mean):
    width = S // NY
    vmem = pl.BlockSpec(memory_space=pltpu.VMEM)
    smem = pl.BlockSpec(memory_space=pltpu.SMEM)
    hbm = pl.BlockSpec(memory_space=pl.ANY)
    f32 = jnp.float32
    dma = pltpu.SemaphoreType.DMA
    inputs = (generator, gates, gain_rows, obs_values, obs_rows)
    both = pl.pallas_call(
        kernel,
        out_shape=jax.ShapeDtypeStruct((2 * STEPS, width), f32),
        in_specs=[hbm] * 5 + [smem, vmem],
        out_specs=vmem,
        scratch_shapes=[pltpu.VMEM(a.shape, a.dtype) for a in inputs]
        + [
            pltpu.VMEM((4, S, S), jnp.bfloat16),
            pltpu.VMEM((STEPS, S), f32),
            pltpu.VMEM((S, S), f32),
            pltpu.VMEM((2, 16, S), f32),
            pltpu.VMEM((STEPS, ROWS, 128), f32),
            pltpu.VMEM((STEPS, ROWS, 128), f32),
            pltpu.VMEM((2, S, S), f32),
            pltpu.VMEM((2, 2, S), f32),
            pltpu.VMEM((2 * PART, S), f32),
            pltpu.VMEM((2 * PART, S), f32),
            pltpu.VMEM((S, S), f32),
            pltpu.VMEM((S, S), f32),
            pltpu.VMEM((QUADS, S, S), f32),
            pltpu.VMEM((2, 2, S), f32),
            pltpu.VMEM((QUADS, 2, 1, S), f32),
            pltpu.VMEM((2, 8, S), f32),
            pltpu.VMEM((NZ, S), f32),
            pltpu.VMEM((NZ, S), f32),
            pltpu.VMEM((2, 8, S), f32),
            pltpu.VMEM((S, S), f32),
            pltpu.VMEM((S, S), f32),
            pltpu.VMEM((S, S), f32),
            dma((5,)),
            dma, dma,
            dma((8,)), dma((8,)),
            dma((4, 2, 2)), dma((4,)),
            dma((4, 4)), dma((4, 4)),
            dma((4, 4)), dma((4, 4)),
            dma((4, 2)), dma((4, 2)),
            dma((2,)), dma((2,)),
        ],
        compiler_params=pltpu.CompilerParams(collective_id=0, has_side_effects=True),
    )(*inputs, obs_counts, prior_mean.reshape(1, S))
    return pl.pallas_call(
        part_results,
        out_shape=[jax.ShapeDtypeStruct((STEPS, width), f32)] * 2,
        in_specs=[vmem],
        out_specs=[vmem] * 2,
    )(both)


def solution(mesh):
    finer = Mesh(mesh.devices.reshape(NX, NZ, NC, NY), TM + ("y",))
    in_specs = (P(), P(TM, None), P(), P(TM, None), P(TM, None), P(TM), P())
    out_specs = (P(TM, "y"), P(TM, "y"))
    return jax.shard_map(shards, mesh=finer, in_specs=in_specs, out_specs=out_specs, check_vma=False)
```

```python
import jax
import jax.numpy as jnp
from jax import lax
from jax.experimental import pallas as pl
from jax.experimental.pallas import tpu as pltpu
from jax.sharding import Mesh
from jax.sharding import PartitionSpec as P

TM = ("x", "z", "c")
NX, NZ, NC, NY = 4, 8, 2, 4
S = 256
STEPS = 16
QUADS = 4
ROWS = S + 8
HALF = S // 2
PART = HALF // 4


def split(x):
    hi = x.astype(jnp.bfloat16)
    return hi, (x - hi.astype(jnp.float32)).astype(jnp.bfloat16)


def mm(a, b):
    return jnp.dot(a, b, preferred_element_type=jnp.float32)


def dot3(a, b):
    ah, al = split(a)
    bh, bl = b
    return mm(ah, bh) + mm(al, bh) + mm(ah, bl)


def eye_mask(rows, columns):
    r = lax.broadcasted_iota(jnp.int32, (rows, columns), 0)
    return r == lax.broadcasted_iota(jnp.int32, (rows, columns), 1)


def to_col(row):
    m = eye_mask(HALF, HALF)
    cols = [jnp.sum(jnp.where(m, row[:, k : k + HALF], 0.0), axis=1, keepdims=True) for k in (0, HALF)]
    return jnp.concatenate(cols, axis=0)


def to_row(col):
    m = eye_mask(HALF, HALF)
    rows = [jnp.sum(jnp.where(m, col[k : k + HALF, :], 0.0), axis=0, keepdims=True) for k in (0, HALF)]
    return jnp.concatenate(rows, axis=1)


def step_on(t, row, add):
    return jnp.sum(t * to_col(row), axis=0, keepdims=True) + add


def step_back(t, row, add):
    return to_row(jnp.sum(t * row, axis=1, keepdims=True)) + add


def kernel(
    gen_hbm, gates_hbm, gain_hbm, vals_hbm, rows_hbm, counts_ref, prior_ref,
    out_ref,
    gen_ref, gates_ref, gain_ref, vals_ref, rows_ref,
    weights, u_s, cur, lines, hist_f, hist_b, pair, slice_vec, lead, own_pair, mate, plane, pair_vec, quad_vec, ends, enter_f, enter_e, chain_out, ahead, behind, total,
    in_sem, send_a, recv_a, send_m, recv_m, send_z, recv_z, send_y, recv_y, send_c, recv_c, send_v, recv_v, send_d, recv_d,
):
    x, z, c, y = (lax.axis_index(a) for a in ("x", "z", "c", "y"))
    sib = 1 - c
    zb = lax.rem(z, 2)
    quad = z // 2
    mate_z = z + 1 - 2 * zb
    above, below, across = (lax.rem(y + k, NY) for k in (1, NY - 1, 2))
    MESH = pl.DeviceIdType.MESH

    def dev(dx=None, dz=None, dc=None, dy=None):
        return tuple(a if d is None else d for a, d in ((x, dx), (z, dz), (c, dc), (y, dy)))

    barrier = pltpu.get_barrier_semaphore()
    partners = [dev(dc=sib), dev(dy=above), dev(dy=below), dev(dy=across)]
    partners += [dev(dz=lax.rem(z + k, NZ)) for k in range(1, NZ)]
    partners += [dev(dx=lax.rem(x + k, NX)) for k in (1, NX - 1)]
    for to in partners:
        pl.semaphore_signal(barrier, inc=1, device_id=to, device_id_type=MESH)

    loads = [
        pltpu.make_async_copy(src, dst, in_sem.at[k])
        for k, (src, dst) in enumerate(
            ((gen_hbm, gen_ref), (rows_hbm, rows_ref), (vals_hbm, vals_ref), (gates_hbm, gates_ref), (gain_hbm, gain_ref))
        )
    ]
    for load in loads:
        load.start()

    loads[0].wait()
    gen = gen_ref[...]
    skew = gen - gen.T
    half_sq = 0.5 * dot3(skew, split(skew))
    eye = jnp.where(eye_mask(S, S), 1.0, 0.0)
    dt = half_sq - skew
    weights[0], weights[1] = split(dt)
    weights[2], weights[3] = split(half_sq + skew)

    lanes = pl.ds(pl.multiple_of((y // 2) * 128, 128), 128)
    loads[3].wait()
    cur[...] = gates_ref[0:1, :] * (eye + dt)
    hist_f[0, 0:S, :] = cur[:, lanes]

    def advance(t, _):
        old = cur[...]
        cur[...] = gates_ref[pl.ds(t, 1), :] * (old + dot3(old, (weights[0], weights[1])))
        hist_f[t, 0:S, :] = cur[:, lanes]
        return 0

    lax.fori_loop(1, STEPS, advance, 0)
    own = pair.at[c]
    own[...] = cur[...]

    pl.semaphore_wait(barrier, len(partners))

    def copy(src, dst, ssem, rsem, to):
        return pltpu.make_async_remote_copy(
            src_ref=src, dst_ref=dst, send_sem=ssem, recv_sem=rsem, device_id=to, device_id_type=MESH
        )

    sent = []

    def go(*args):
        d = copy(*args)
        d.start()
        sent.append(d)

    swap = copy(own, own, send_a, recv_a, dev(dc=sib))
    swap.start()
    sent.append(swap)
    loads[1].wait()
    loads[2].wait()
    slots = vals_ref.shape[1]
    sensors = gain_ref.shape[0]
    lane = lax.broadcasted_iota(jnp.int32, (STEPS, slots), 1)
    line = lax.broadcasted_iota(jnp.int32, (STEPS, slots), 0)
    count = jnp.zeros((STEPS, slots), jnp.int32)
    for t in range(STEPS):
        count = jnp.where(line == t, counts_ref[t], count)
    vals = jnp.where(lane < count, vals_ref[...], 0.0)
    rows = rows_ref[...]
    ids = lax.broadcasted_iota(jnp.int32, (STEPS, sensors), 1)
    w = jnp.zeros((STEPS, sensors), jnp.float32)
    for s in range(slots):
        w = w + jnp.where(rows[:, s : s + 1] == ids, vals[:, s : s + 1], 0.0)
    loads[4].wait()
    u_s[...] = dot3(w, split(gain_ref[...]))

    lines[...] = jnp.zeros((2, 16, S), jnp.float32)

    def affine(k, _):
        g = gates_ref[pl.ds(k, 1), :]
        f = lines[0]
        f = g * (f + dot3(f, (weights[0], weights[1]))) + u_s[pl.ds(k, 1), :]
        lines[0] = f
        hist_f[k, S : S + 8, :] = lines[0, 0:8, lanes]
        t = STEPS - 1 - k
        e = (lines[1] + u_s[pl.ds(t, 1), :]) * gates_ref[pl.ds(t, 1), :]
        lines[1] = e + dot3(e, (weights[2], weights[3]))
        hist_b[lax.rem(t + STEPS - 1, STEPS), S : S + 8, :] = lines[1, 0:8, lanes]
        return 0

    lax.fori_loop(0, 4, affine, 0)
    swap.wait_recv()
    base = pl.multiple_of(c * HALF, HALF)

    kinds = (y, above, below, across)

    def rows_of(kind):
        return pl.ds(pl.multiple_of(c * HALF + kinds[kind] * PART, PART), PART)

    def to_mate(kind):
        return copy(
            own_pair.at[rows_of(kind), :], mate.at[rows_of(kind), :], send_m.at[kind], recv_m.at[kind], dev(dz=mate_z)
        )

    lead[...] = dot3(pair[0, rows_of(0), :], split(pair[1]))
    first_rows = copy(lead, mate.at[rows_of(0), :], send_m.at[0], recv_m.at[0], dev(dz=mate_z))
    first_rows.start()
    sent.append(first_rows)
    own_pair[...] = dot3(pair[0], split(pair[1]))
    lax.fori_loop(4, 10, affine, 0)

    first_rows.wait_recv()

    def others(act):
        for dq, to_b in ((0, 0), (1, 0), (3, 1), (1, 1), (3, 0), (2, 0), (2, 1)):
            act(dev(dz=lax.rem(2 * quad + 2 * dq, NZ) + to_b), dq, to_b)

    def quad_rows(q, kind):
        return plane.at[q, rows_of(kind), :]

    def spread(to, dq, to_b):
        ref = quad_rows(quad, 0)
        return copy(ref, ref, send_z.at[dq, to_b], recv_z.at[(4 - dq) % 4], to)

    @pl.when(zb == 1)
    def _():
        plane[quad, rows_of(0), :] = dot3(mate[rows_of(0), :], split(own_pair[...]))
        others(lambda *a: spread(*a).start())

    lax.fori_loop(10, STEPS, affine, 0)
    slice_vec[c, 0:1, :] = lines[0, 0:1, :]
    slice_vec[c, 1:2, :] = lines[1, 0:1, :]
    swap_slice = copy(slice_vec.at[c], slice_vec.at[c], send_m.at[6], recv_m.at[6], dev(dc=sib))
    swap_slice.start()
    sent.append(swap_slice)

    swap_slice.wait_recv()
    pair_vec[zb, 0:1, :] = step_on(pair[1], slice_vec[0, 0:1, :], slice_vec[1, 0:1, :])
    pair_vec[zb, 1:2, :] = step_back(pair[0], slice_vec[1, 1:2, :], slice_vec[0, 1:2, :])
    swap_vec = copy(pair_vec.at[zb], pair_vec.at[zb], send_m.at[4], recv_m.at[4], dev(dz=mate_z))
    swap_vec.start()
    sent.append(swap_vec)

    def arrive(r):
        q = lax.rem(quad + r, QUADS)
        ref = quad_rows(q, 0)
        wait = copy(ref, ref, send_z.at[0, 0], recv_z.at[r], dev(dz=mate_z)).wait_recv
        if r:
            wait()
        else:
            pl.when(zb == 0)(wait)
        for kind, to in ((3, across), (2, above), (1, below)):
            go(ref, ref, send_y.at[r, kind], recv_y.at[r, kind], dev(dy=to))
        go(ref, ref, send_c.at[r, 0], recv_c.at[r, 0], dev(dc=sib))

    def arrive_y(r):
        q = lax.rem(quad + r, QUADS)
        for kind in (1, 2, 3):
            ref = quad_rows(q, kind)
            copy(ref, ref, send_y.at[r, kind], recv_y.at[r, kind], dev(dy=above)).wait_recv()
            go(ref, ref, send_c.at[r, kind], recv_c.at[r, kind], dev(dc=sib))

    arrive(0)
    arrive(3)

    swap_vec.wait_recv()

    @pl.when(zb == 1)
    def _():
        quad_vec[quad, 0] = step_on(own_pair[...], pair_vec[0, 0:1, :], pair_vec[1, 0:1, :])

    @pl.when(zb == 0)
    def _():
        quad_vec[quad, 1] = step_back(own_pair[...], pair_vec[1, 1:2, :], pair_vec[0, 1:2, :])

    def spread_vec(to_z, dq, far):
        ref = quad_vec.at[quad, 1 - zb]
        return copy(ref, ref, send_v.at[dq, far], recv_v.at[(4 - dq) % 4, 1 - zb], dev(dz=to_z))

    for dq in range(QUADS):
        for far in (0, 1):
            if dq or not far:
                d = spread_vec(mate_z if dq == 0 else lax.rem(2 * quad + 2 * dq, NZ) + far, dq, far)
                d.start()
                sent.append(d)
    arrive(1)
    arrive_y(0)
    arrive(2)

    for kind in (1, 2, 3):
        d = to_mate(kind)
        d.start()
        sent.append(d)
    arrive_y(3)
    arrive_y(1)
    arrive_y(2)
    for r in range(QUADS):
        for kind in range(4):
            ref = quad_rows(0, 0)
            copy(ref, ref, send_c.at[r, kind], recv_c.at[r, kind], dev(dc=sib)).wait_recv()
    for r in range(QUADS):
        for kind in (0, 1) if r else (zb,):
            v = quad_vec.at[quad, 0]
            copy(v, v, send_v.at[0, 0], recv_v.at[r, kind], dev(dz=mate_z)).wait_recv()

    def chain(way):
        to = dev(dx=lax.rem(x + (NX - 1 if way else 1), NX))
        return copy(chain_out.at[way], ends.at[way], send_d.at[way], recv_d.at[way], to)

    zero = jnp.zeros((1, S), jnp.float32)
    f_row = jnp.where(x == 0, prior_ref[...], zero)
    e_row = zero
    for k in range(QUADS):
        enter_f[k : k + 1, :] = f_row
        f_row = step_on(plane[k], f_row, quad_vec[k, 0])
        n = QUADS - 1 - k
        enter_e[n : n + 1, :] = e_row
        e_row = step_back(plane[n], e_row, quad_vec[n, 1])
    chain_out[0] = f_row
    chain_out[1] = e_row

    @pl.when(x == 0)
    def _():
        chain(0).start()

    @pl.when(x == NX - 1)
    def _():
        chain(1).start()

    for kind in (1, 2, 3):
        to_mate(kind).wait_recv()
    half_mate = mate.at[pl.ds(base, HALF), :]
    go(half_mate, half_mate, send_m.at[5], recv_m.at[5], dev(dc=sib))

    total[...] = plane[0]
    ahead[...] = eye

    def compose(k, _):
        @pl.when(k == quad)
        def _():
            ahead[...] = total[...]

        total[...] = dot3(total[...], split(plane[k]))
        return 0

    lax.fori_loop(1, QUADS, compose, 0)

    def pass_on(way):
        chain(way).wait_recv()
        row = ends[way, 0:1, :]
        new = (step_back if way else step_on)(total[...], row, chain_out[way, 0:1, :])
        chain_out[way] = new
        chain(way).start()

    behind[...] = eye

    @pl.when(quad < QUADS - 1)
    def _():
        behind[...] = plane[lax.rem(quad + 1, QUADS)]

    def compose_after(k, _):
        behind[...] = dot3(behind[...], split(plane[k]))
        return 0

    lax.fori_loop(jnp.minimum(quad + 2, QUADS), QUADS, compose_after, 0)

    @pl.when(x == 1)
    def _():
        pass_on(0)

    @pl.when(x == 2)
    def _():
        pass_on(1)

    copy(half_mate, half_mate, send_m.at[5], recv_m.at[5], dev(dc=sib)).wait_recv()

    @pl.when(zb == 1)
    def _():
        ahead[...] = dot3(ahead[...], split(mate[...]))

    @pl.when(c == 1)
    def _():
        ahead[...] = dot3(ahead[...], split(pair[0]))

    @pl.when(zb == 0)
    def _():
        behind[...] = dot3(mate[...], split(behind[...]))

    @pl.when(c == 0)
    def _():
        behind[...] = dot3(pair[1], split(behind[...]))

    f_off = enter_f[pl.ds(quad, 1), :]
    f_off = jnp.where(zb == 1, step_on(mate[...], f_off, pair_vec[0, 0:1, :]), f_off)
    f_off = jnp.where(c == 1, step_on(pair[0], f_off, slice_vec[0, 0:1, :]), f_off)
    e_off = enter_e[pl.ds(quad, 1), :]
    e_off = jnp.where(zb == 0, step_back(mate[...], e_off, pair_vec[1, 1:2, :]), e_off)
    e_off = jnp.where(c == 0, step_back(pair[1], e_off, slice_vec[1, 1:2, :]), e_off)

    cur[...] = eye

    def retreat(k, _):
        t = STEPS - 1 - k
        old = cur[...] * gates_ref[pl.ds(t, 1), :]
        cur[...] = old + dot3(old, (weights[2], weights[3]))
        hist_b[t - 1, 0:S, :] = cur[:, lanes]
        return 0

    lax.fori_loop(0, 5, retreat, 0)

    @pl.when(x == 1)
    def _():
        pass_on(1)

    @pl.when(x == 2)
    def _():
        pass_on(0)

    lax.fori_loop(5, STEPS - 1, retreat, 0)

    @pl.when(x == 0)
    def _():
        chain(1).wait_recv()
        ends[0] = jnp.zeros((1, S), jnp.float32)

    @pl.when(x == NX - 1)
    def _():
        chain(0).wait_recv()
        ends[1] = jnp.zeros((1, S), jnp.float32)

    f_in = step_on(ahead[...], ends[0, 0:1, :], f_off)
    e_in = step_back(behind[...], ends[1, 0:1, :], e_off)
    f_col = to_col(f_in)
    e_col = to_col(e_in)
    width = S // NY
    low = lax.rem(y, 2) == 0
    e_last = jnp.where(y < 2, e_in[:, 0:128], e_in[:, 128:])

    def pick(r):
        return jnp.where(low, r[:, 0:width], r[:, width:])

    for t in range(STEPS):
        f = jnp.sum(hist_f[t, 0:S, :] * f_col, axis=0, keepdims=True) + hist_f[t, S : S + 1, :]
        if t < STEPS - 1:
            e = jnp.sum(hist_b[t, 0:S, :] * e_col, axis=0, keepdims=True) + hist_b[t, S : S + 1, :]
        else:
            e = e_last
        out_ref[t : t + 1, :] = pick(f)
        out_ref[STEPS + t : STEPS + t + 1, :] = pick(f + e)

    for d in sent:
        d.wait_send()

    @pl.when(zb == 1)
    def _():
        others(lambda *a: spread(*a).wait_send())

    @pl.when(x < NX - 1)
    def _():
        chain(0).wait_send()

    @pl.when(x > 0)
    def _():
        chain(1).wait_send()


def part_results(both_ref, filt_ref, smooth_ref):
    filt_ref[...] = both_ref[0:STEPS, :]
    smooth_ref[...] = both_ref[STEPS:, :]


def shards(generator, gates, gain_rows, obs_values, obs_rows, obs_counts, prior_mean):
    width = S // NY
    vmem = pl.BlockSpec(memory_space=pltpu.VMEM)
    smem = pl.BlockSpec(memory_space=pltpu.SMEM)
    hbm = pl.BlockSpec(memory_space=pl.ANY)
    f32 = jnp.float32
    dma = pltpu.SemaphoreType.DMA
    inputs = (generator, gates, gain_rows, obs_values, obs_rows)
    both = pl.pallas_call(
        kernel,
        out_shape=jax.ShapeDtypeStruct((2 * STEPS, width), f32),
        in_specs=[hbm] * 5 + [smem, vmem],
        out_specs=vmem,
        scratch_shapes=[pltpu.VMEM(a.shape, a.dtype) for a in inputs]
        + [
            pltpu.VMEM((4, S, S), jnp.bfloat16),
            pltpu.VMEM((STEPS, S), f32),
            pltpu.VMEM((S, S), f32),
            pltpu.VMEM((2, 16, S), f32),
            pltpu.VMEM((STEPS, ROWS, 128), f32),
            pltpu.VMEM((STEPS, ROWS, 128), f32),
            pltpu.VMEM((2, S, S), f32),
            pltpu.VMEM((2, 2, S), f32),
            pltpu.VMEM((PART, S), f32),
            pltpu.VMEM((S, S), f32),
            pltpu.VMEM((S, S), f32),
            pltpu.VMEM((QUADS, S, S), f32),
            pltpu.VMEM((2, 2, S), f32),
            pltpu.VMEM((QUADS, 2, 1, S), f32),
            pltpu.VMEM((2, 1, S), f32),
            pltpu.VMEM((NZ, S), f32),
            pltpu.VMEM((NZ, S), f32),
            pltpu.VMEM((2, 1, S), f32),
            pltpu.VMEM((S, S), f32),
            pltpu.VMEM((S, S), f32),
            pltpu.VMEM((S, S), f32),
            dma((5,)),
            dma, dma,
            dma((7,)), dma((7,)),
            dma((4, 2)), dma((4,)),
            dma((4, 4)), dma((4, 4)),
            dma((4, 4)), dma((4, 4)),
            dma((4, 2)), dma((4, 2)),
            dma((2,)), dma((2,)),
        ],
        compiler_params=pltpu.CompilerParams(collective_id=0, has_side_effects=True),
    )(*inputs, obs_counts, prior_mean.reshape(1, S))
    return pl.pallas_call(
        part_results,
        out_shape=[jax.ShapeDtypeStruct((STEPS, width), f32)] * 2,
        in_specs=[vmem],
        out_specs=[vmem] * 2,
    )(both)


def solution(mesh):
    finer = Mesh(mesh.devices.reshape(NX, NZ, NC, NY), TM + ("y",))
    in_specs = (P(), P(TM, None), P(), P(TM, None), P(TM, None), P(TM), P())
    out_specs = (P(TM, "y"), P(TM, "y"))
    return jax.shard_map(shards, mesh=finer, in_specs=in_specs, out_specs=out_specs, check_vma=False)
```

```python
import jax
import jax.numpy as jnp
from jax import lax
from jax.experimental import pallas as pl
from jax.experimental.pallas import tpu as pltpu
from jax.sharding import Mesh
from jax.sharding import PartitionSpec as P

TM = ("x", "z", "c")
NX, NZ, NC, NY = 4, 8, 2, 4
S = 256
STEPS = 16
QUADS = 4
ROWS = S + 8
HALF = S // 2
PART = HALF // 4


def split(x):
    hi = x.astype(jnp.bfloat16)
    return hi, (x - hi.astype(jnp.float32)).astype(jnp.bfloat16)


def mm(a, b):
    return jnp.dot(a, b, preferred_element_type=jnp.float32)


def dot3(a, b):
    ah, al = split(a)
    bh, bl = b
    return mm(ah, bh) + mm(al, bh) + mm(ah, bl)


def eye_mask(rows, columns):
    r = lax.broadcasted_iota(jnp.int32, (rows, columns), 0)
    return r == lax.broadcasted_iota(jnp.int32, (rows, columns), 1)


def to_col(row):
    m = eye_mask(HALF, HALF)
    cols = [jnp.sum(jnp.where(m, row[:, k : k + HALF], 0.0), axis=1, keepdims=True) for k in (0, HALF)]
    return jnp.concatenate(cols, axis=0)


def to_row(col):
    m = eye_mask(HALF, HALF)
    rows = [jnp.sum(jnp.where(m, col[k : k + HALF, :], 0.0), axis=0, keepdims=True) for k in (0, HALF)]
    return jnp.concatenate(rows, axis=1)


def step_on(t, row, add):
    return jnp.sum(t * to_col(row), axis=0, keepdims=True) + add


def step_back(t, row, add):
    return to_row(jnp.sum(t * row, axis=1, keepdims=True)) + add


def kernel(
    gen_hbm, gates_hbm, gain_hbm, vals_hbm, rows_hbm, counts_ref, prior_ref,
    out_ref,
    gen_ref, gates_ref, gain_ref, vals_ref, rows_ref,
    weights, u_s, cur, lines, hist_f, hist_b, pair, slice_vec, lead, own_pair, mate, plane, pair_vec, quad_vec, ends, enter_f, enter_e, chain_out, ahead, behind, total, steps_f, steps_e,
    in_sem, send_a, recv_a, send_m, recv_m, send_z, recv_z, send_y, recv_y, send_c, recv_c, send_v, recv_v, send_d, recv_d,
):
    x, z, c, y = (lax.axis_index(a) for a in ("x", "z", "c", "y"))
    sib = 1 - c
    zb = lax.rem(z, 2)
    quad = z // 2
    mate_z = z + 1 - 2 * zb
    above, below, across = (lax.rem(y + k, NY) for k in (1, NY - 1, 2))
    MESH = pl.DeviceIdType.MESH

    def dev(dx=None, dz=None, dc=None, dy=None):
        return tuple(a if d is None else d for a, d in ((x, dx), (z, dz), (c, dc), (y, dy)))

    barrier = pltpu.get_barrier_semaphore()
    partners = [dev(dc=sib), dev(dy=above), dev(dy=below), dev(dy=across)]
    partners += [dev(dz=lax.rem(z + k, NZ)) for k in range(1, NZ)]
    partners += [dev(dx=lax.rem(x + k, NX)) for k in (1, NX - 1)]
    for to in partners:
        pl.semaphore_signal(barrier, inc=1, device_id=to, device_id_type=MESH)

    loads = [
        pltpu.make_async_copy(src, dst, in_sem.at[k])
        for k, (src, dst) in enumerate(
            ((gen_hbm, gen_ref), (rows_hbm, rows_ref), (vals_hbm, vals_ref), (gates_hbm, gates_ref), (gain_hbm, gain_ref))
        )
    ]
    for load in loads:
        load.start()

    loads[0].wait()
    gen = gen_ref[...]
    skew = gen - gen.T
    half_sq = 0.5 * dot3(skew, split(skew))
    eye = jnp.where(eye_mask(S, S), 1.0, 0.0)
    dt = half_sq - skew
    weights[0], weights[1] = split(dt)
    weights[2], weights[3] = split(half_sq + skew)

    lanes = pl.ds(pl.multiple_of((y // 2) * 128, 128), 128)
    loads[3].wait()
    cur[...] = gates_ref[0:1, :] * (eye + dt)
    hist_f[0, 0:S, :] = cur[:, lanes]

    def advance(t, _):
        old = cur[...]
        cur[...] = gates_ref[pl.ds(t, 1), :] * (old + dot3(old, (weights[0], weights[1])))
        hist_f[t, 0:S, :] = cur[:, lanes]
        return 0

    lax.fori_loop(1, STEPS, advance, 0)
    own = pair.at[c]
    own[...] = cur[...]

    pl.semaphore_wait(barrier, len(partners))

    def copy(src, dst, ssem, rsem, to):
        return pltpu.make_async_remote_copy(
            src_ref=src, dst_ref=dst, send_sem=ssem, recv_sem=rsem, device_id=to, device_id_type=MESH
        )

    sent = []

    def go(*args):
        d = copy(*args)
        d.start()
        sent.append(d)

    swap = copy(own, own, send_a, recv_a, dev(dc=sib))
    swap.start()
    sent.append(swap)
    loads[1].wait()
    loads[2].wait()
    slots = vals_ref.shape[1]
    sensors = gain_ref.shape[0]
    lane = lax.broadcasted_iota(jnp.int32, (STEPS, slots), 1)
    line = lax.broadcasted_iota(jnp.int32, (STEPS, slots), 0)
    count = jnp.zeros((STEPS, slots), jnp.int32)
    for t in range(STEPS):
        count = jnp.where(line == t, counts_ref[t], count)
    vals = jnp.where(lane < count, vals_ref[...], 0.0)
    rows = rows_ref[...]
    ids = lax.broadcasted_iota(jnp.int32, (STEPS, sensors), 1)
    w = jnp.zeros((STEPS, sensors), jnp.float32)
    for s in range(slots):
        w = w + jnp.where(rows[:, s : s + 1] == ids, vals[:, s : s + 1], 0.0)
    loads[4].wait()
    u_s[...] = dot3(w, split(gain_ref[...]))

    lines[...] = jnp.zeros((2, 16, S), jnp.float32)

    def affine(k, _):
        g = gates_ref[pl.ds(k, 1), :]
        f = lines[0]
        f = g * (f + dot3(f, (weights[0], weights[1]))) + u_s[pl.ds(k, 1), :]
        lines[0] = f
        hist_f[k, S : S + 8, :] = lines[0, 0:8, lanes]
        t = STEPS - 1 - k
        e = (lines[1] + u_s[pl.ds(t, 1), :]) * gates_ref[pl.ds(t, 1), :]
        lines[1] = e + dot3(e, (weights[2], weights[3]))
        hist_b[lax.rem(t + STEPS - 1, STEPS), S : S + 8, :] = lines[1, 0:8, lanes]
        return 0

    lax.fori_loop(0, 4, affine, 0)
    swap.wait_recv()
    base = pl.multiple_of(c * HALF, HALF)

    kinds = (y, above, below, across)

    def rows_of(kind):
        return pl.ds(pl.multiple_of(c * HALF + kinds[kind] * PART, PART), PART)

    def to_mate(kind):
        return copy(
            own_pair.at[rows_of(kind), :], mate.at[rows_of(kind), :], send_m.at[kind], recv_m.at[kind], dev(dz=mate_z)
        )

    lead[...] = dot3(pair[0, rows_of(0), :], split(pair[1]))
    first_rows = copy(lead, mate.at[rows_of(0), :], send_m.at[0], recv_m.at[0], dev(dz=mate_z))
    first_rows.start()
    sent.append(first_rows)
    own_pair[...] = dot3(pair[0], split(pair[1]))
    lax.fori_loop(4, 10, affine, 0)

    first_rows.wait_recv()

    def others(act):
        for dq, to_b in ((0, 0), (1, 0), (3, 1), (1, 1), (3, 0), (2, 0), (2, 1)):
            act(dev(dz=lax.rem(2 * quad + 2 * dq, NZ) + to_b), dq, to_b)

    def quad_rows(q, kind):
        return plane.at[q, rows_of(kind), :]

    def spread(to, dq, to_b):
        ref = quad_rows(quad, 0)
        return copy(ref, ref, send_z.at[dq, to_b], recv_z.at[(4 - dq) % 4], to)

    @pl.when(zb == 1)
    def _():
        plane[quad, rows_of(0), :] = dot3(mate[rows_of(0), :], split(own_pair[...]))
        others(lambda *a: spread(*a).start())

    lax.fori_loop(10, STEPS, affine, 0)
    slice_vec[c, 0:1, :] = lines[0, 0:1, :]
    slice_vec[c, 1:2, :] = lines[1, 0:1, :]
    swap_slice = copy(slice_vec.at[c], slice_vec.at[c], send_m.at[6], recv_m.at[6], dev(dc=sib))
    swap_slice.start()
    sent.append(swap_slice)

    swap_slice.wait_recv()
    pair_vec[zb, 0:1, :] = step_on(pair[1], slice_vec[0, 0:1, :], slice_vec[1, 0:1, :])
    pair_vec[zb, 1:2, :] = step_back(pair[0], slice_vec[1, 1:2, :], slice_vec[0, 1:2, :])
    swap_vec = copy(pair_vec.at[zb], pair_vec.at[zb], send_m.at[4], recv_m.at[4], dev(dz=mate_z))
    swap_vec.start()
    sent.append(swap_vec)

    def arrive(r):
        q = lax.rem(quad + r, QUADS)
        ref = quad_rows(q, 0)
        wait = copy(ref, ref, send_z.at[0, 0], recv_z.at[r], dev(dz=mate_z)).wait_recv
        if r:
            wait()
        else:
            pl.when(zb == 0)(wait)
        for kind, to in ((3, across), (2, above), (1, below)):
            go(ref, ref, send_y.at[r, kind], recv_y.at[r, kind], dev(dy=to))
        go(ref, ref, send_c.at[r, 0], recv_c.at[r, 0], dev(dc=sib))

    def arrive_y(r):
        q = lax.rem(quad + r, QUADS)
        for kind in (1, 2, 3):
            ref = quad_rows(q, kind)
            copy(ref, ref, send_y.at[r, kind], recv_y.at[r, kind], dev(dy=above)).wait_recv()
            go(ref, ref, send_c.at[r, kind], recv_c.at[r, kind], dev(dc=sib))

    arrive(0)
    arrive(3)

    swap_vec.wait_recv()

    @pl.when(zb == 1)
    def _():
        quad_vec[quad, 0] = step_on(own_pair[...], pair_vec[0, 0:1, :], pair_vec[1, 0:1, :])

    @pl.when(zb == 0)
    def _():
        quad_vec[quad, 1] = step_back(own_pair[...], pair_vec[1, 1:2, :], pair_vec[0, 1:2, :])

    def spread_vec(to_z, dq, far):
        ref = quad_vec.at[quad, 1 - zb]
        return copy(ref, ref, send_v.at[dq, far], recv_v.at[(4 - dq) % 4, 1 - zb], dev(dz=to_z))

    for dq in range(QUADS):
        for far in (0, 1):
            if dq or not far:
                d = spread_vec(mate_z if dq == 0 else lax.rem(2 * quad + 2 * dq, NZ) + far, dq, far)
                d.start()
                sent.append(d)
    arrive(1)
    arrive_y(0)
    arrive(2)

    for kind in (1, 2, 3):
        d = to_mate(kind)
        d.start()
        sent.append(d)
    arrive_y(3)
    arrive_y(1)
    arrive_y(2)
    for r in range(QUADS):
        for kind in range(4):
            ref = quad_rows(0, 0)
            copy(ref, ref, send_c.at[r, kind], recv_c.at[r, kind], dev(dc=sib)).wait_recv()
    for r in range(QUADS):
        for kind in (0, 1) if r else (zb,):
            v = quad_vec.at[quad, 0]
            copy(v, v, send_v.at[0, 0], recv_v.at[r, kind], dev(dz=mate_z)).wait_recv()

    def chain(way):
        to = dev(dx=lax.rem(x + (NX - 1 if way else 1), NX))
        return copy(chain_out.at[way], ends.at[way], send_d.at[way], recv_d.at[way], to)

    zero = jnp.zeros((1, S), jnp.float32)
    f_row = jnp.where(x == 0, prior_ref[...], zero)
    e_row = zero
    for k in range(QUADS):
        enter_f[k : k + 1, :] = f_row
        f_row = step_on(plane[k], f_row, quad_vec[k, 0])
        n = QUADS - 1 - k
        enter_e[n : n + 1, :] = e_row
        e_row = step_back(plane[n], e_row, quad_vec[n, 1])
    chain_out[0] = f_row
    chain_out[1] = e_row

    @pl.when(x == 0)
    def _():
        chain(0).start()

    @pl.when(x == NX - 1)
    def _():
        chain(1).start()

    for kind in (1, 2, 3):
        to_mate(kind).wait_recv()
    half_mate = mate.at[pl.ds(base, HALF), :]
    go(half_mate, half_mate, send_m.at[5], recv_m.at[5], dev(dc=sib))

    total[...] = plane[0]
    ahead[...] = eye

    def compose(k, _):
        @pl.when(k == quad)
        def _():
            ahead[...] = total[...]

        total[...] = dot3(total[...], split(plane[k]))
        return 0

    lax.fori_loop(1, QUADS, compose, 0)

    def pass_on(way):
        chain(way).wait_recv()
        row = ends[way, 0:1, :]
        new = (step_back if way else step_on)(total[...], row, chain_out[way, 0:1, :])
        chain_out[way] = new
        chain(way).start()

    behind[...] = eye

    @pl.when(quad < QUADS - 1)
    def _():
        behind[...] = plane[lax.rem(quad + 1, QUADS)]

    def compose_after(k, _):
        behind[...] = dot3(behind[...], split(plane[k]))
        return 0

    lax.fori_loop(jnp.minimum(quad + 2, QUADS), QUADS, compose_after, 0)

    @pl.when(x == 1)
    def _():
        pass_on(0)

    @pl.when(x == 2)
    def _():
        pass_on(1)

    copy(half_mate, half_mate, send_m.at[5], recv_m.at[5], dev(dc=sib)).wait_recv()

    @pl.when(zb == 1)
    def _():
        ahead[...] = dot3(ahead[...], split(mate[...]))

    @pl.when(c == 1)
    def _():
        ahead[...] = dot3(ahead[...], split(pair[0]))

    @pl.when(zb == 0)
    def _():
        behind[...] = dot3(mate[...], split(behind[...]))

    @pl.when(c == 0)
    def _():
        behind[...] = dot3(pair[1], split(behind[...]))

    f_off = enter_f[pl.ds(quad, 1), :]
    f_off = jnp.where(zb == 1, step_on(mate[...], f_off, pair_vec[0, 0:1, :]), f_off)
    f_off = jnp.where(c == 1, step_on(pair[0], f_off, slice_vec[0, 0:1, :]), f_off)
    e_off = enter_e[pl.ds(quad, 1), :]
    e_off = jnp.where(zb == 0, step_back(mate[...], e_off, pair_vec[1, 1:2, :]), e_off)
    e_off = jnp.where(c == 0, step_back(pair[1], e_off, slice_vec[1, 1:2, :]), e_off)

    cur[...] = eye

    def retreat(k, _):
        t = STEPS - 1 - k
        old = cur[...] * gates_ref[pl.ds(t, 1), :]
        cur[...] = old + dot3(old, (weights[2], weights[3]))
        hist_b[t - 1, 0:S, :] = cur[:, lanes]
        return 0

    lax.fori_loop(0, 5, retreat, 0)

    @pl.when(x == 1)
    def _():
        pass_on(1)

    @pl.when(x == 2)
    def _():
        pass_on(0)

    lax.fori_loop(5, STEPS - 1, retreat, 0)

    def make_f():
        f_in = step_on(ahead[...], ends[0, 0:1, :], f_off)
        col = to_col(f_in)
        for t in range(STEPS):
            steps_f[t : t + 1, :] = jnp.sum(hist_f[t, 0:S, :] * col, axis=0, keepdims=True) + hist_f[t, S : S + 1, :]

    def make_e():
        e_in = step_back(behind[...], ends[1, 0:1, :], e_off)
        col = to_col(e_in)
        for t in range(STEPS - 1):
            steps_e[t : t + 1, :] = jnp.sum(hist_b[t, 0:S, :] * col, axis=0, keepdims=True) + hist_b[t, S : S + 1, :]
        steps_e[STEPS - 1 : STEPS, :] = jnp.where(y < 2, e_in[:, 0:128], e_in[:, 128:])

    @pl.when(x == 0)
    def _():
        ends[0] = jnp.zeros((1, S), jnp.float32)

    @pl.when(x == NX - 1)
    def _():
        ends[1] = jnp.zeros((1, S), jnp.float32)

    @pl.when(x < 2)
    def _():
        make_f()

        @pl.when(x == 0)
        def _():
            chain(1).wait_recv()

        make_e()

    @pl.when(x >= 2)
    def _():
        make_e()

        @pl.when(x == NX - 1)
        def _():
            chain(0).wait_recv()

        make_f()

    width = S // NY
    low = lax.rem(y, 2) == 0

    def pick(r):
        return jnp.where(low, r[:, 0:width], r[:, width:])

    out_ref[0:STEPS, :] = pick(steps_f[...])
    out_ref[STEPS:, :] = pick(steps_f[...] + steps_e[...])

    for d in sent:
        d.wait_send()

    @pl.when(zb == 1)
    def _():
        others(lambda *a: spread(*a).wait_send())

    @pl.when(x < NX - 1)
    def _():
        chain(0).wait_send()

    @pl.when(x > 0)
    def _():
        chain(1).wait_send()


def part_results(both_ref, filt_ref, smooth_ref):
    filt_ref[...] = both_ref[0:STEPS, :]
    smooth_ref[...] = both_ref[STEPS:, :]


def shards(generator, gates, gain_rows, obs_values, obs_rows, obs_counts, prior_mean):
    width = S // NY
    vmem = pl.BlockSpec(memory_space=pltpu.VMEM)
    smem = pl.BlockSpec(memory_space=pltpu.SMEM)
    hbm = pl.BlockSpec(memory_space=pl.ANY)
    f32 = jnp.float32
    dma = pltpu.SemaphoreType.DMA
    inputs = (generator, gates, gain_rows, obs_values, obs_rows)
    both = pl.pallas_call(
        kernel,
        out_shape=jax.ShapeDtypeStruct((2 * STEPS, width), f32),
        in_specs=[hbm] * 5 + [smem, vmem],
        out_specs=vmem,
        scratch_shapes=[pltpu.VMEM(a.shape, a.dtype) for a in inputs]
        + [
            pltpu.VMEM((4, S, S), jnp.bfloat16),
            pltpu.VMEM((STEPS, S), f32),
            pltpu.VMEM((S, S), f32),
            pltpu.VMEM((2, 16, S), f32),
            pltpu.VMEM((STEPS, ROWS, 128), f32),
            pltpu.VMEM((STEPS, ROWS, 128), f32),
            pltpu.VMEM((2, S, S), f32),
            pltpu.VMEM((2, 2, S), f32),
            pltpu.VMEM((PART, S), f32),
            pltpu.VMEM((S, S), f32),
            pltpu.VMEM((S, S), f32),
            pltpu.VMEM((QUADS, S, S), f32),
            pltpu.VMEM((2, 2, S), f32),
            pltpu.VMEM((QUADS, 2, 1, S), f32),
            pltpu.VMEM((2, 1, S), f32),
            pltpu.VMEM((NZ, S), f32),
            pltpu.VMEM((NZ, S), f32),
            pltpu.VMEM((2, 1, S), f32),
            pltpu.VMEM((S, S), f32),
            pltpu.VMEM((S, S), f32),
            pltpu.VMEM((S, S), f32),
            pltpu.VMEM((STEPS, 128), f32),
            pltpu.VMEM((STEPS, 128), f32),
            dma((5,)),
            dma, dma,
            dma((7,)), dma((7,)),
            dma((4, 2)), dma((4,)),
            dma((4, 4)), dma((4, 4)),
            dma((4, 4)), dma((4, 4)),
            dma((4, 2)), dma((4, 2)),
            dma((2,)), dma((2,)),
        ],
        compiler_params=pltpu.CompilerParams(collective_id=0, has_side_effects=True),
    )(*inputs, obs_counts, prior_mean.reshape(1, S))
    return pl.pallas_call(
        part_results,
        out_shape=[jax.ShapeDtypeStruct((STEPS, width), f32)] * 2,
        in_specs=[vmem],
        out_specs=[vmem] * 2,
    )(both)


def solution(mesh):
    finer = Mesh(mesh.devices.reshape(NX, NZ, NC, NY), TM + ("y",))
    in_specs = (P(), P(TM, None), P(), P(TM, None), P(TM, None), P(TM), P())
    out_specs = (P(TM, "y"), P(TM, "y"))
    return jax.shard_map(shards, mesh=finer, in_specs=in_specs, out_specs=out_specs, check_vma=False)
```
